256 devices in a mesh: sect: 2 (over core), grp: 16 (over y_hi, z), tp: 8 (over y_lo, x).
Axes of the slice: x: 4, y: 4 (y_hi: 2, y_lo: 2; y = y_hi * 2 + y_lo), z: 8, core: 2. Of those that a mesh axis runs over, the one named last changes fastest.
Arguments:
- queries: bfloat16 [512, 128, 576], P('grp', ('sect', 'tp')), may hold values from -400 to 400, as said below
- latent_cache: bfloat16 [512, 128, 576], P('grp'), may hold values from -6 to 6, as said below
- cache_len: int32 [512], P('grp'), may hold values from 1 to 128, 32768 in all
- value_up: bfloat16 [128, 512, 128], P(('sect', 'tp')), may hold values from -0.25 to 0.25
- out_proj: bfloat16 [16384, 7168], P(('sect', 'tp'), 'grp'), may hold values from -0.046875 to 0.046875
- residual: bfloat16 [512, 7168], P(None, 'grp'), may hold values from -3 to 3
- w_gate: bfloat16 [16, 7168, 2048], P('grp', None, ('sect', 'tp')), may hold values from -0.0625 to 0.0625
- w_up: bfloat16 [16, 7168, 2048], P('grp', None, ('sect', 'tp')), may hold values from -0.0625 to 0.0625
- w_down: bfloat16 [16, 2048, 7168], P('grp', ('sect', 'tp')), may hold values from -0.1875 to 0.1875
- route_ids: int32 [512, 8], replicated, may hold values from 0 to 15, all different within a row; in each aligned block of 512 rows (0 to 511, 512 to 1023, ...) at most 384 rows name the same one
- route_weights: float32 [512, 8], replicated, may hold values from 0.1 to 0.6
Outputs:
- layer_out: bfloat16 [512, 7168], P(('sect', 'tp'), 'grp')
The draws below stay inside these ranges and needn't reach their ends.
Inputs may be any that keep to these rules, and one draw needn't show every extreme that they name: `queries`: every entry lies in this range. `latent_cache`: every entry lies in this range. `route_ids`: each row names 8 different experts; every expert is named by at most 384 rows, and one expert by exactly 384. `cache_len`: some row has exactly 128 filled positions.
All inputs are finite; a program needn't handle non-finite values. No bound on the sum of `cache_len` on one device may be relied on, other than what follows from the above.
Results may differ from the reference program's by a relative error of at most 0.018.
Values may be sent and summed in bfloat16 or wider, within the bound.
A program may use at most 128 MiB of HBM per device.

```python
import math
import jax
import jax.numpy as jnp
import numpy as np
from jax import lax

D = 7168
HEADS = 128
LAT = 512
ROPE = 64
VDIM = 128
FF = 2048
TOP = 8
CACHE = 128
ROWS = 512
EXPERTS = 16
CAP = 384


def attention_inputs(key):
    cache_key = jax.random.fold_in(key, 11)
    query_key = jax.random.fold_in(key, 23)
    latents = jax.random.truncated_normal(cache_key, -6.0, 6.0, (ROWS, CACHE, LAT + ROPE), jnp.float32)
    query_vals = jax.random.truncated_normal(query_key, -6.0, 6.0, (ROWS, HEADS, LAT + ROPE), jnp.float32)
    return (query_vals, latents)


def draw_queries(key, part):
    query_vals, latents = attention_inputs(key)
    return query_vals.astype(jnp.bfloat16)


def draw_latent_cache(key, part):
    query_vals, latents = attention_inputs(key)
    return latents.astype(jnp.bfloat16)


def strengthened(values, stream_key, source, target, blocks, factor):
    owner, partner = [(jnp.arange(values.shape[axis_at]) // (values.shape[axis_at] // blocks)).reshape([-1 if axis == axis_at else 1 for axis in range(values.ndim)]) for axis_at in (source, target)]
    chosen = jax.random.permutation(stream_key, blocks)[partner]
    strong = (owner == chosen) | (owner == (partner + blocks // 2) % blocks)
    return jnp.where(strong, factor * values, values)


def steps_of(stream_key, dims, pieces, low, top_value):
    def one(position, blocks):
        draws = jax.random.uniform(jax.random.fold_in(jax.random.fold_in(stream_key, 6), position), (blocks,), jnp.float32, low / len(pieces), top_value / len(pieces))
        return jnp.repeat(jnp.exp(draws), dims[position] // blocks).reshape((-1,) + (1,) * (len(dims) - position - 1))

    gain = one(*pieces[0])
    for cut in pieces[1:]:
        gain = gain * one(*cut)
    return gain


def length_profile(amount, total, limit, skew):
    weights = [(1 << 20) // math.isqrt(rank ** skew) + 1 for rank in range(2, amount + 1)]
    rest, counts = total - limit - (amount - 1), [1] * (amount - 1)
    while rest > 0:
        movable = [i for i in range(amount - 1) if counts[i] < limit]
        pool, left = sum([weights[i] for i in movable]), rest
        for i in movable:
            extra = min(limit - counts[i], max(1, left * weights[i] // pool), rest)
            counts[i] = counts[i] + extra
            rest = rest - extra
    return np.array([limit] + counts)


def uneven(stream_key, count, total, bound, slope):
    if count == 2:
        one = jax.random.randint(stream_key, (), max(1, total - bound), min(bound, total - 1) + 1)
        return jnp.stack([one, total - one])
    sizes = jnp.asarray(length_profile(count, total, bound, slope), jnp.int32)
    pairs = (count - 1) // 2
    giver, receiver = sizes[1:1 + 2 * pairs:2], sizes[2:2 + 2 * pairs:2]
    room = jnp.minimum(giver - 1, bound - receiver)
    moved = jax.random.randint(jax.random.fold_in(stream_key, 1), (pairs,), 0, 1 << 20) % (room + 1)
    sizes = sizes.at[1:1 + 2 * pairs:2].set(giver - moved).at[2:2 + 2 * pairs:2].set(receiver + moved)
    return sizes[jax.random.permutation(jax.random.fold_in(stream_key, 2), count)]


def assign_block(stream_key, own, number, rows, amount, top, reach, skew):
    ranking = jax.random.permutation(stream_key, amount)
    packed, ordinary = portions_of(amount, rows * top, reach, skew, True), portions_of(amount, rows * top, reach, skew, False)
    places = jnp.arange(amount)

    def named(sizes, turn):
        used = int((sizes > 0).sum())
        fixed = max(1, used // 4)
        passed = fixed + (places - fixed + turn * (used - fixed)) % max(1, amount - fixed)
        return jnp.zeros((amount,), jnp.int32).at[ranking[jnp.where(places < fixed, places, passed)]].set(jnp.asarray(sizes, jnp.int32))

    sizes = jnp.where(number % 4 == 0, named(packed, number // 4), named(ordinary, number - number // 4 - 1))
    mixed = jax.random.permutation(jax.random.fold_in(own, 3), amount)
    giver, sink = mixed[0:amount // 2 * 2:2], mixed[1:amount // 2 * 2:2]
    slack = jnp.minimum(sizes[giver] - 1, reach - sizes[sink]) // 2
    slack = jnp.where((giver == ranking[0]) | (sink == ranking[0]) | (sizes[sink] == 0), 0, jnp.maximum(slack, 0))
    passed = jax.random.randint(jax.random.fold_in(own, 4), (amount // 2,), 0, 1 << 20) % (slack + 1)
    sizes = sizes.at[giver].add(-passed).at[sink].add(passed)
    items = jnp.searchsorted(jnp.cumsum(sizes), jnp.arange(rows * top), side="right").astype(jnp.int32)
    table = items.reshape(top, rows).T
    table = table[jax.random.permutation(jax.random.fold_in(own, 1), rows)]
    turn = jax.random.randint(jax.random.fold_in(own, 2), (rows, 1), 0, top)
    return jnp.take_along_axis(table, (jnp.arange(top)[None, :] + turn) % top, axis=1)


def portions_of(amount, total, reach, slope, full):
    weights = [(1 << 20) // math.isqrt(rank ** slope) + 1 for rank in range(1, amount + 1)]
    largest = reach if full else min(reach, max(-(-total // amount), total * weights[0] // sum(weights)))
    least = 1 if total - largest >= amount - 1 else 0
    holding, surplus = [largest] + [least] * (amount - 1), total - largest - least * (amount - 1)
    while surplus > 0:
        free = [i for i in range(1, amount) if holding[i] < largest] or [i for i in range(1, amount) if holding[i] < reach]
        whole, left = sum([weights[i] for i in free]), surplus
        for i in free:
            more = min(reach - holding[i], max(1, left * weights[i] // whole), surplus)
            holding[i] = holding[i] + more
            surplus = surplus - more
    return np.array(holding)


def normal_values(own_key, dims, spread, reach, pieces=(), held_as=jnp.bfloat16):
    factor_of = steps_of(own_key, dims, pieces, -0.22, 0.18) if pieces else 1.0
    drawn = jax.random.normal(own_key, dims, jnp.float32) * spread * factor_of
    return jnp.minimum(jnp.maximum(drawn, -reach), reach).astype(held_as)


def heavy_noise(rng, extent, spread, limit, cuts, heavy, kind=jnp.bfloat16):
    values = spread * jax.random.normal(rng, extent, jnp.float32)
    if cuts:
        values = values * steps_of(rng, extent, cuts, -0.22, 0.18)
    return jnp.clip(strengthened(values, jax.random.fold_in(rng, 3), *heavy), -limit, limit).astype(kind)


def setup_inputs(seed: int = 0) -> dict:
    keys = jax.random.split(jax.random.key(seed), 12)
    queries = draw_queries(jax.random.fold_in(keys[11], 71), 0)
    latent_cache = draw_latent_cache(jax.random.fold_in(keys[11], 71), 0)
    cache_len = uneven(keys[2], ROWS, ROWS * CACHE // 2, CACHE, 2).astype(jnp.int32)
    value_up = normal_values(keys[3], (HEADS, LAT, VDIM), LAT ** -0.5, 0.25, ((0, 16),))
    out_proj = normal_values(keys[4], (HEADS * VDIM, D), (HEADS * VDIM) ** -0.5, 0.046875, ((0, 16), (1, 16)))
    residual = normal_values(keys[5], (ROWS, D), 0.5, 3.0, ((1, 16),))
    w_gate = normal_values(keys[6], (EXPERTS, D, FF), D ** -0.5, 0.0625, ((0, 16), (2, 16)))
    w_up = normal_values(keys[7], (EXPERTS, D, FF), D ** -0.5, 0.0625, ((0, 16), (2, 16)))
    w_down = heavy_noise(keys[8], (EXPERTS, FF, D), FF ** -0.5, 0.1875, ((0, 16), (1, 16)), (0, 2, 16, 2.0))
    route_ids_keys = jax.random.split(jax.random.fold_in(keys[9], 1), ROWS // ROWS)
    route_ids_turns = jax.random.permutation(jax.random.fold_in(keys[9], 3), ROWS // ROWS)
    route_ids = jax.vmap(lambda own, number: assign_block(jax.random.fold_in(keys[9], 2), own, number, ROWS, EXPERTS, TOP, CAP, 2))(route_ids_keys, route_ids_turns).reshape((ROWS, TOP))
    route_weights = jnp.clip(jnp.exp(jax.random.uniform(keys[10], (ROWS, TOP), jnp.float32, math.log(0.1), math.log(0.6))), 0.1, 0.6)
    return dict(queries=queries, latent_cache=latent_cache, cache_len=cache_len, value_up=value_up, out_proj=out_proj, residual=residual, w_gate=w_gate, w_up=w_up, w_down=w_down, route_ids=route_ids, route_weights=route_weights)


SOFTMAX_SCALE = 0.0721688
MASK_VALUE = -1e30


def reference(queries, latent_cache, cache_len, value_up, out_proj, residual, w_gate, w_up, w_down, route_ids, route_weights):
    query_f = queries.astype(jnp.float32)
    cache_f = latent_cache.astype(jnp.float32)
    scores = jnp.einsum("rhk,rlk->rhl", query_f, cache_f) * SOFTMAX_SCALE
    positions = jnp.arange(CACHE, dtype=jnp.int32)
    in_range = positions[None, None, :] < cache_len[:, None, None]
    masked = jnp.where(in_range, scores, MASK_VALUE)
    row_max = jnp.max(masked, axis=2, keepdims=True)
    exp_scores = jnp.where(in_range, jnp.exp(masked - row_max), 0.0)
    probs = (exp_scores / jnp.sum(exp_scores, axis=2, keepdims=True)).astype(jnp.bfloat16)
    latent_out = jnp.einsum("rhl,rlc->rhc", probs.astype(jnp.float32), cache_f[:, :, :LAT]).astype(jnp.bfloat16)
    heads_out = jnp.einsum("rhc,hcv->rhv", latent_out.astype(jnp.float32), value_up.astype(jnp.float32))
    heads_out = heads_out.astype(jnp.bfloat16).reshape(ROWS, HEADS * VDIM)
    attention = jnp.dot(heads_out, out_proj, preferred_element_type=jnp.float32)
    layer_input = (residual.astype(jnp.float32) + attention).astype(jnp.bfloat16)

    def expert_step(running, expert_index):
        matches = route_ids == expert_index
        weight = jnp.sum(jnp.where(matches, route_weights, 0.0), axis=1)
        gate_value = jnp.dot(layer_input, w_gate[expert_index], preferred_element_type=jnp.float32)
        up_value = jnp.dot(layer_input, w_up[expert_index], preferred_element_type=jnp.float32)
        hidden = (weight[:, None] * jax.nn.silu(gate_value) * up_value).astype(jnp.bfloat16)
        return running + jnp.dot(hidden, w_down[expert_index], preferred_element_type=jnp.float32), None

    routed, _ = lax.scan(expert_step, jnp.zeros((ROWS, D), jnp.float32), jnp.arange(EXPERTS, dtype=jnp.int32))
    return (layer_input.astype(jnp.float32) + routed).astype(jnp.bfloat16)
```

```python
import jax
import jax.numpy as jnp
from jax import lax
from jax.experimental import pallas as pl
from jax.experimental.pallas import tpu as pltpu
from jax.sharding import PartitionSpec as P

LAT = 512
VDIM = 128
NX = 4
NY = 4
NZ = 8
NT = 8
NG = 16
NST = 16
BR = 32
BC = 448

SOFTMAX_SCALE = 0.0721688
MASK_VALUE = -1e30
MESH = pl.DeviceIdType.MESH
BF16 = jnp.bfloat16
F32 = jnp.float32


def _here():
    s = lax.axis_index("sect")
    g = lax.axis_index("grp")
    t = lax.axis_index("tp")
    yh, z = g // NZ, g % NZ
    yl, x = t // NX, t % NX
    return s, g, t, yh, z, yl, x


def _remote(src, dst, send, recv, dev):
    return pltpu.make_async_remote_copy(
        src_ref=src, dst_ref=dst, send_sem=send, recv_sem=recv, device_id=dev, device_id_type=MESH
    )


def _signal_all(devs):
    barrier = pltpu.get_barrier_semaphore()
    for dev in devs:
        pl.semaphore_signal(barrier, inc=1, device_id=dev, device_id_type=MESH)
    pl.semaphore_wait(barrier, len(devs))


def _heads_kernel(own_ref, out_ref, send_sem, psend_sem, recv_sem, local_sem):
    s, g, t, yh, z, yl, x = _here()
    oh = 1 - yh
    right = {"grp": yh * NZ + (z + 1) % NZ}
    left = {"grp": yh * NZ + (z + NZ - 1) % NZ}
    across = {"grp": oh * NZ + z}
    _signal_all([right, left, across])

    def hop(src, slot, way):
        c = _remote(src, out_ref.at[slot], send_sem.at[slot, way], recv_sem.at[slot], (right, left)[way])
        c.start()
        sent.append(c)

    def landed(slot):
        _remote(own_ref, out_ref.at[slot], psend_sem, recv_sem.at[slot], right).wait_recv()

    sent = []
    keep = pltpu.make_async_copy(own_ref, out_ref.at[g], local_sem)
    keep.start()
    pc = _remote(own_ref, out_ref.at[g], psend_sem, recv_sem.at[g], across)
    pc.start()
    hop(own_ref, g, 0)
    hop(own_ref, g, 1)
    half = NZ // 2

    def near(k):
        slot = yh * NZ + (z + NZ - k) % NZ
        landed(slot)
        if k < half:
            hop(out_ref.at[slot], slot, 0)
        if k < half:
            slot = yh * NZ + (z + k) % NZ
            landed(slot)
            if k < half - 1:
                hop(out_ref.at[slot], slot, 1)

    def far(k):
        if k == 0:
            slot = oh * NZ + z
            landed(slot)
            hop(out_ref.at[slot], slot, 0)
            hop(out_ref.at[slot], slot, 1)
            return
        if k < half:
            slot = oh * NZ + (z + NZ - k) % NZ
            landed(slot)
            if k < half - 1:
                hop(out_ref.at[slot], slot, 0)
        slot = oh * NZ + (z + k) % NZ
        landed(slot)
        if k < half:
            hop(out_ref.at[slot], slot, 1)

    for k in range(half + 1):
        if k < half:
            near(k + 1)
        far(k)
    keep.wait()
    pc.wait_send()
    for c in sent:
        c.wait_send()


def gather_heads(heads):
    out = pl.pallas_call(
        _heads_kernel,
        out_shape=jax.ShapeDtypeStruct((NG,) + heads.shape, BF16),
        in_specs=[pl.BlockSpec(memory_space=pltpu.VMEM)],
        out_specs=pl.BlockSpec(memory_space=pltpu.VMEM),
        scratch_shapes=[
            pltpu.SemaphoreType.DMA((NG, 2)),
            pltpu.SemaphoreType.DMA,
            pltpu.SemaphoreType.DMA((NG,)),
            pltpu.SemaphoreType.DMA,
        ],
        compiler_params=pltpu.CompilerParams(collective_id=0, has_side_effects=True),
        name="gather_heads",
    )(heads)
    return out.reshape(NG * heads.shape[0], heads.shape[1])


def _spread_kernel(
    part_ref, res_ref, all_ref, own_ref, rbuf, bsend, brecv, ssend, srecv, ysend, yrecv, rsend, rrecv, psend, precv
):
    s, g, t, yh, z, yl, x = _here()
    y = yh * 2 + yl
    d = s * NT + t

    def st_dev(e):
        return {"sect": e // NT, "tp": e % NT}

    def y_dev(e):
        return {"grp": (e // 2) * NZ + z, "tp": (e % 2) * NX + x}

    def z_dev(e):
        return {"grp": yh * NZ + e}

    def x_dev(e):
        return {"tp": yl * NX + e}

    partner = {"sect": 1 - s}
    _signal_all(
        [st_dev((d + o) % NST) for o in range(1, NST)]
        + [z_dev((z + o) % NZ) for o in range(1, NZ)]
        + [y_dev((y + o) % NY) for o in range(1, NY)]
    )

    sent = []

    def start(c):
        c.start()
        sent.append(c)

    for o in range(1, NST):
        e = (d + o) % NST
        start(_remote(part_ref.at[e], rbuf.at[d], bsend.at[o], brecv.at[d], st_dev(e)))
    total = res_ref[...].astype(F32) + part_ref[d].astype(F32)
    for o in range(1, NST):
        e = (d + NST - o) % NST
        _remote(part_ref.at[e], rbuf.at[e], bsend.at[o], brecv.at[e], st_dev(e)).wait_recv()
        total = total + rbuf[e].astype(F32)
    mine = total.astype(BF16)
    own_ref[...] = mine
    all_ref[yh, z, s, t] = mine

    def wait_recv(ref, sem):
        _remote(ref, ref, psend.at[0], sem, partner).wait_recv()

    @pl.when(s == 0)
    def _():
        def piece(xx, yy):
            return all_ref.at[yy // 2, :, 0, (yy % 2) * NX + xx]

        mark = len(sent)
        block = all_ref.at[yh, z, 0, t]
        for o in range(1, NZ):
            start(_remote(block, block, ssend.at[o], srecv.at[z], z_dev((z + o) % NZ)))
        for o in range(1, NZ):
            e = (z + NZ - o) % NZ
            wait_recv(all_ref.at[yh, e, 0, t], srecv.at[e])

        def to_partner(p, i):
            start(_remote(p, p, psend.at[i], precv.at[i], partner))

        xr, xl = (x + 1) % NX, (x + NX - 1) % NX
        xo = (x + 2) % NX
        order = (0, 3, 1, 2)
        for o in order[1:]:
            p = piece(x, y)
            start(_remote(p, p, ysend.at[o], yrecv.at[o], y_dev((y + o) % NY)))
        for j, o in enumerate(order):
            p = piece(x, (y + NY - o) % NY)
            if o:
                wait_recv(p, yrecv.at[o])
            start(_remote(p, p, rsend.at[0, j], rrecv.at[0, j], x_dev(xr)))
            start(_remote(p, p, rsend.at[1, j], rrecv.at[1, j], x_dev(xl)))
            to_partner(p, j)
        for j, o in enumerate(order):
            yy = (y + NY - o) % NY
            p = piece(xl, yy)
            wait_recv(p, rrecv.at[0, j])
            if j % 2 == 0:
                start(_remote(p, p, rsend.at[2, j], rrecv.at[2, j], x_dev(xr)))
            to_partner(p, 4 + j)
            p = piece(xr, yy)
            wait_recv(p, rrecv.at[1, j])
            if j % 2 == 1:
                start(_remote(p, p, rsend.at[2, j], rrecv.at[2, j], x_dev(xl)))
            to_partner(p, 8 + j)
        for j, o in enumerate(order):
            p = piece(xo, (y + NY - o) % NY)
            wait_recv(p, rrecv.at[2, j])
            to_partner(p, 12 + j)
        for c in sent[mark:]:
            c.wait_send()
        del sent[mark:]

    @pl.when(s == 1)
    def _():
        def piece(zz, hh):
            return all_ref.at[hh, zz, 1]

        mark = len(sent)
        block = all_ref.at[yh, z, 1, t]
        for o in range(1, NX):
            start(_remote(block, block, ssend.at[o], srecv.at[o], x_dev((x + o) % NX)))
        for o in range(1, NX):
            e = (x + NX - o) % NX
            wait_recv(all_ref.at[yh, z, 1, yl * NX + e], srecv.at[o])

        def quad(yy):
            return all_ref.at[yy // 2, z, 1, pl.ds((yy % 2) * NX, NX)]

        for o in range(1, NY):
            p = quad(y)
            start(_remote(p, p, ysend.at[o], yrecv.at[o], y_dev((y + o) % NY)))
        for o in range(1, NY):
            wait_recv(quad((y + NY - o) % NY), yrecv.at[o])

        def to_partner(p, i):
            start(_remote(p, p, psend.at[i], precv.at[i], partner))

        zr, zl = (z + 1) % NZ, (z + NZ - 1) % NZ
        half = NZ // 2
        for h in range(2):
            p = piece(z, h)
            start(_remote(p, p, rsend.at[0, h], rrecv.at[0, h], z_dev(zr)))
            start(_remote(p, p, rsend.at[1, h], rrecv.at[1, h], z_dev(zl)))
            to_partner(p, h)
        for k in range(1, half):
            for h in range(2):
                p = piece((z + NZ - k) % NZ, h)
                wait_recv(p, rrecv.at[0, 2 * (k - 1) + h])
                if k < half - 1 or h == 0:
                    start(_remote(p, p, rsend.at[0, 2 * k + h], rrecv.at[0, 2 * k + h], z_dev(zr)))
                to_partner(p, 4 * k - 2 + h)
                p = piece((z + k) % NZ, h)
                wait_recv(p, rrecv.at[1, 2 * (k - 1) + h])
                if k < half - 1 or h == 1:
                    start(_remote(p, p, rsend.at[1, 2 * k + h], rrecv.at[1, 2 * k + h], z_dev(zl)))
                to_partner(p, 4 * k + h)
        for h in range(2):
            p = piece((z + half) % NZ, h)
            wait_recv(p, rrecv.at[h, 2 * (half - 1) + h])
            to_partner(p, 14 + h)
        for c in sent[mark:]:
            c.wait_send()
        del sent[mark:]

    for c in sent:
        c.wait_send()

    @pl.when(s == 0)
    def _():
        for i in range(2):
            wait_recv(all_ref.at[i, z, 1], precv.at[i])
        for k in range(1, NZ // 2):
            for h in range(2):
                wait_recv(all_ref.at[h, (z + NZ - k) % NZ, 1], precv.at[4 * k - 2 + h])
                wait_recv(all_ref.at[h, (z + k) % NZ, 1], precv.at[4 * k + h])
        for h in range(2):
            wait_recv(all_ref.at[h, (z + NZ // 2) % NZ, 1], precv.at[14 + h])

    @pl.when(s == 1)
    def _():
        for i, xx in enumerate((x, (x + NX - 1) % NX, (x + 1) % NX, (x + 2) % NX)):
            for j, o in enumerate((0, 3, 1, 2)):
                yy = (y + NY - o) % NY
                wait_recv(all_ref.at[yy // 2, :, 0, (yy % 2) * NX + xx], precv.at[4 * i + j])


def spread_rows(partial, residual):
    vmem = pl.BlockSpec(memory_space=pltpu.VMEM)
    dma = pltpu.SemaphoreType.DMA
    everything, own = pl.pallas_call(
        _spread_kernel,
        out_shape=(
            jax.ShapeDtypeStruct((2, NZ, 2, NT, BR, BC), BF16),
            jax.ShapeDtypeStruct((BR, BC), BF16),
        ),
        in_specs=[vmem, vmem],
        out_specs=(vmem, vmem),
        scratch_shapes=[
            pltpu.VMEM((NST, BR, BC), BF16),
            dma((NST,)),
            dma((NST,)),
            dma((NZ,)),
            dma((NZ,)),
            dma((NY,)),
            dma((NY,)),
            dma((3, NZ)),
            dma((3, NZ)),
            dma((16,)),
            dma((16,)),
        ],
        compiler_params=pltpu.CompilerParams(
            collective_id=1, has_side_effects=True, vmem_limit_bytes=32 * 1024 * 1024
        ),
        name="spread_rows",
    )(partial.reshape(NST, BR, BC), residual)
    return everything.reshape(NG, NST * BR, BC), own


def _expert_kernel(g_ref, x_ref, wg_ref, wu_ref, wd_ref, ids_ref, wts_ref, out_ref, acc_ref, hid_ref):
    i = pl.program_id(0)

    @pl.when(i == 0)
    def _():
        acc_ref[...] = jnp.zeros_like(acc_ref)

    @pl.when(i < NG)
    def _():
        w = jnp.concatenate([wg_ref[...], wu_ref[...]], axis=1)
        acc_ref[...] += jnp.dot(x_ref[0], w, preferred_element_type=F32)

    @pl.when(i == NG)
    def _():
        g = g_ref[0]
        weight = jnp.sum(jnp.where(ids_ref[...] == g, wts_ref[...], 0.0), axis=1, keepdims=True)
        gate = acc_ref[:, :128]
        up = acc_ref[:, 128:]
        hid_ref[...] = (weight * (gate / (1.0 + jnp.exp(-gate))) * up).astype(BF16)

    @pl.when((i >= NG) & (i % 2 == 0))
    def _():
        out_ref[0] = jnp.dot(hid_ref[...], wd_ref[:, :BC], preferred_element_type=F32).astype(BF16)

    @pl.when((i >= NG) & (i % 2 == 1))
    def _():
        out_ref[0] = jnp.dot(hid_ref[...], wd_ref[:, BC:], preferred_element_type=F32).astype(BF16)


def expert_terms(rows, w_gate, w_up, w_down, route_ids, route_weights):
    own = lax.axis_index("grp").astype(jnp.int32).reshape(1)
    n = rows.shape[1]
    grid_spec = pltpu.PrefetchScalarGridSpec(
        num_scalar_prefetch=1,
        grid=(2 * NG,),
        in_specs=[
            pl.BlockSpec((1, n, BC), lambda i, o: (jnp.minimum(i, NG - 1), 0, 0)),
            pl.BlockSpec((BC, 128), lambda i, o: (jnp.minimum(i, NG - 1), 0)),
            pl.BlockSpec((BC, 128), lambda i, o: (jnp.minimum(i, NG - 1), 0)),
            pl.BlockSpec((128, 2 * BC), lambda i, o: (0, jnp.maximum(i - NG, 0) // 2)),
            pl.BlockSpec((n, 8), lambda i, o: (0, 0)),
            pl.BlockSpec((n, 8), lambda i, o: (0, 0)),
        ],
        out_specs=pl.BlockSpec((1, n, BC), lambda i, o: (jnp.maximum(i - NG, 0), 0, 0)),
        scratch_shapes=[pltpu.VMEM((n, 256), F32), pltpu.VMEM((n, 128), BF16)],
    )
    return pl.pallas_call(
        _expert_kernel,
        out_shape=jax.ShapeDtypeStruct((NG, n, BC), BF16),
        grid_spec=grid_spec,
        compiler_params=pltpu.CompilerParams(vmem_limit_bytes=32 * 1024 * 1024),
        name="expert_terms",
    )(own, rows, w_gate, w_up, w_down, route_ids, route_weights)


def _combine_kernel(
    term_ref, own_ref, out_ref, pbuf, acc, ring, ybuf, fbuf, psend, precv, rsend, rrecv, ysend, yrecv, fsend, frecv
):
    s, g, t, yh, z, yl, x = _here()
    y = yh * 2 + yl

    def y_dev(e):
        return {"grp": (e // 2) * NZ + z, "tp": (e % 2) * NX + x}

    def z_dev(e):
        return {"grp": yh * NZ + e}

    def x_dev(e):
        return {"tp": yl * NX + e}

    partner = {"sect": 1 - s}
    _signal_all(
        [partner]
        + [x_dev((x + o) % NX) for o in range(1, NX)]
        + [y_dev((y + o) % NY) for o in range(1, NY)]
        + [z_dev((z + o) % NZ) for o in range(1, NZ)]
    )
    sent = []

    def start(c):
        c.start()
        sent.append(c)

    def wait_recv(ref, sem):
        _remote(ref, ref, psend.at[0], sem, partner).wait_recv()

    def add(dst, srcs, n=8):
        def step(i, carry):
            v = srcs[0][i].astype(F32)
            for r in srcs[1:]:
                v = v + r[i].astype(F32)
            dst[i] = v.astype(BF16)
            return carry

        lax.fori_loop(0, n, step, 0)

    def finish(pairs):
        v = own_ref[...].astype(F32)
        tot = None
        for r in pairs:
            w = r[...].astype(F32)
            tot = w if tot is None else tot + w
        out_ref[...] = (v + tot).astype(BF16)

    xs = ((x + 2) % NX, (x + 1) % NX, (x + NX - 1) % NX, x)
    zs = [(z + NZ // 2) % NZ]
    for k in range(NZ // 2 - 1, 0, -1):
        zs += [(z + k) % NZ, (z + NZ - k) % NZ]
    zs.append(z)
    ys = ((y + 2) % NY, (y + 1) % NY, (y + NY - 1) % NY, y)

    @pl.when(s == 0)
    def _():
        for i, zz in enumerate(zs):
            for h in range(2):
                start(
                    _remote(
                        term_ref.at[h, zz, 1], pbuf.at[h, zz], psend.at[2 * i + h], precv.at[2 * i + h], partner
                    )
                )

        def at(ref, i, j):
            yy = ys[j]
            return ref.at[yy // 2, :, (yy % 2) * NX + xs[i]]

        def own_part(i, j, more=()):
            yy = ys[j]
            wait_recv(at(pbuf, i, j), precv.at[4 * i + j])
            add(
                at(acc, i, j),
                [term_ref.at[yy // 2, :, 0, (yy % 2) * NX + xs[i]], at(pbuf, i, j)] + list(more),
            )

        mark = 0
        right, left = x_dev((x + 1) % NX), x_dev((x + NX - 1) % NX)
        for j in range(4):
            own_part(0, j)
            start(_remote(at(acc, 0, j), ring.at[j], rsend.at[j], rrecv.at[j], right if j % 2 == 0 else left))
        for j in range(4):
            for i, way, dev in ((1, 0, right), (2, 1, left)):
                if j % 2 == way:
                    wait_recv(ring.at[j], rrecv.at[j])
                    own_part(i, j, [ring.at[j]])
                else:
                    own_part(i, j)
                k = 4 + 4 * way + j
                start(_remote(at(acc, i, j), ring.at[k], rsend.at[k], rrecv.at[k], dev))
        for j in range(4):
            wait_recv(ring.at[4 + j], rrecv.at[4 + j])
            wait_recv(ring.at[8 + j], rrecv.at[8 + j])
            if j < 3:
                own_part(3, j, [ring.at[4 + j], ring.at[8 + j]])
                o = (2, 1, 3)[j]
                start(_remote(at(acc, 3, j), ybuf.at[o], ysend.at[o], yrecv.at[o], y_dev(ys[j])))
            else:
                for o in (2, 1, 3):
                    wait_recv(ybuf.at[o], yrecv.at[o])
                own_part(3, j, [ring.at[4 + j], ring.at[8 + j]] + [ybuf.at[o] for o in (2, 1, 3)])
        for o in range(1, NZ):
            e = (z + o) % NZ
            start(_remote(acc.at[yh, e, t], fbuf.at[o], fsend.at[o], frecv.at[o], z_dev(e)))
        for o in range(1, NZ):
            wait_recv(fbuf.at[o], frecv.at[o])
        finish([acc.at[yh, z, t]] + [fbuf.at[o] for o in range(1, NZ)])
        for c in sent[mark:]:
            c.wait_send()
        del sent[mark:]

    @pl.when(s == 1)
    def _():
        for i, xx in enumerate(xs):
            for j, yy in enumerate(ys):
                r = (yy // 2, slice(None), 0, (yy % 2) * NX + xx)
                start(
                    _remote(
                        term_ref.at[r],
                        pbuf.at[yy // 2, :, (yy % 2) * NX + xx],
                        psend.at[4 * i + j],
                        precv.at[4 * i + j],
                        partner,
                    )
                )

        def own_part(i, h, more=()):
            zz = zs[i]
            wait_recv(pbuf.at[h, zz], precv.at[2 * i + h])
            add(acc.at[h, zz], [term_ref.at[h, zz, 1], pbuf.at[h, zz]] + list(more))

        right, left = z_dev((z + 1) % NZ), z_dev((z + NZ - 1) % NZ)
        for h in range(2):
            own_part(0, h)
            start(_remote(acc.at[h, zs[0]], ring.at[h], rsend.at[h], rrecv.at[h], (right, left)[h]))
        for k in range(1, NZ // 2):
            for h in range(2):
                for way, dev in ((0, right), (1, left)):
                    i = 2 * k - 1 + way
                    prev = None
                    if k == 1:
                        if h == way:
                            prev = h
                    else:
                        prev = 2 + 4 * (k - 2) + 2 * way + h
                    if prev is None:
                        own_part(i, h)
                    else:
                        wait_recv(ring.at[prev], rrecv.at[prev])
                        own_part(i, h, [ring.at[prev]])
                    q = 2 + 4 * (k - 1) + 2 * way + h
                    start(_remote(acc.at[h, zs[i]], ring.at[q], rsend.at[q], rrecv.at[q], dev))
        for h in range(2):
            q = 2 + 4 * (NZ // 2 - 2) + h
            wait_recv(ring.at[q], rrecv.at[q])
            wait_recv(ring.at[q + 2], rrecv.at[q + 2])
            own_part(7, h, [ring.at[q], ring.at[q + 2]])

        def quad(yy):
            return acc.at[yy // 2, z, pl.ds((yy % 2) * NX, NX)]

        def qbuf(o):
            return ybuf.at[o, pl.ds(0, NX)]

        for o in (2, 1, 3):
            e = (y + o) % NY
            start(_remote(quad(e), qbuf(o), ysend.at[o], yrecv.at[o], y_dev(e)))
        for o in (2, 1, 3):
            wait_recv(qbuf(o), yrecv.at[o])
        add(quad(y), [quad(y)] + [qbuf(o) for o in (2, 1, 3)], NX)
        for o in range(1, NX):
            e = (x + o) % NX
            start(_remote(acc.at[yh, z, yl * NX + e], fbuf.at[o], fsend.at[o], frecv.at[o], x_dev(e)))
        for o in range(1, NX):
            wait_recv(fbuf.at[o], frecv.at[o])
        finish([acc.at[yh, z, t]] + [fbuf.at[o] for o in range(1, NX)])
        for c in sent:
            c.wait_send()


def combine_terms(terms, own):
    vmem = pl.BlockSpec(memory_space=pltpu.VMEM)
    dma = pltpu.SemaphoreType.DMA
    return pl.pallas_call(
        _combine_kernel,
        out_shape=jax.ShapeDtypeStruct((BR, BC), BF16),
        in_specs=[vmem, vmem],
        out_specs=vmem,
        scratch_shapes=[
            pltpu.VMEM((2, NZ, NT, BR, BC), BF16),
            pltpu.VMEM((2, NZ, NT, BR, BC), BF16),
            pltpu.VMEM((16, 8, BR, BC), BF16),
            pltpu.VMEM((4, 8, BR, BC), BF16),
            pltpu.VMEM((8, BR, BC), BF16),
            dma((16,)),
            dma((16,)),
            dma((16,)),
            dma((16,)),
            dma((4,)),
            dma((4,)),
            dma((8,)),
            dma((8,)),
        ],
        compiler_params=pltpu.CompilerParams(
            collective_id=2, has_side_effects=True, vmem_limit_bytes=48 * 1024 * 1024
        ),
        name="combine_terms",
    )(terms.reshape(2, NZ, 2, NT, BR, BC), own)


def on_device(
    queries,
    latent_cache,
    cache_len,
    value_up,
    out_proj,
    residual,
    w_gate,
    w_up,
    w_down,
    route_ids,
    route_weights,
):
    local_rows = queries.shape[0]
    local_heads = queries.shape[1]
    scores = (
        jnp.einsum("rhk,rlk->rhl", queries, latent_cache, preferred_element_type=F32) * SOFTMAX_SCALE
    )
    positions = jnp.arange(latent_cache.shape[1], dtype=jnp.int32)
    in_range = positions[None, None, :] < cache_len[:, None, None]
    masked = jnp.where(in_range, scores, MASK_VALUE)
    row_max = jnp.max(masked, axis=2, keepdims=True)
    exp_scores = jnp.where(in_range, jnp.exp(masked - row_max), 0.0)
    probs = (exp_scores / jnp.sum(exp_scores, axis=2, keepdims=True)).astype(BF16)
    latent_out = jnp.einsum(
        "rhl,rlc->rhc", probs, latent_cache[:, :, :LAT], preferred_element_type=F32
    ).astype(BF16)
    heads_out = jnp.einsum("rhc,hcv->rhv", latent_out, value_up, preferred_element_type=F32)
    heads_out = heads_out.astype(BF16).reshape(local_rows, local_heads * VDIM)
    partial_attn = jnp.dot(gather_heads(heads_out), out_proj, preferred_element_type=F32).astype(BF16)
    tensor_index = lax.axis_index(("sect", "tp"))
    own_residual = lax.dynamic_slice_in_dim(residual, tensor_index * BR, BR, 0)
    rows, own_rows = spread_rows(partial_attn, own_residual)
    terms = expert_terms(rows, w_gate[0], w_up[0], w_down[0], route_ids, route_weights)
    return combine_terms(terms, own_rows)


def solution(mesh):
    return jax.shard_map(
        on_device,
        mesh=mesh,
        in_specs=(
            P("grp", ("sect", "tp"), None),
            P("grp", None, None),
            P("grp"),
            P(("sect", "tp"), None, None),
            P(("sect", "tp"), "grp"),
            P(None, "grp"),
            P("grp", None, ("sect", "tp")),
            P("grp", None, ("sect", "tp")),
            P("grp", ("sect", "tp"), None),
            P(),
            P(),
        ),
        out_specs=P(("sect", "tp"), "grp"),
        check_vma=False,
    )
```

```python
import jax
import jax.numpy as jnp
from jax import lax
from jax.experimental import pallas as pl
from jax.experimental.pallas import tpu as pltpu
from jax.sharding import PartitionSpec as P

LAT = 512
VDIM = 128
NX = 4
NY = 4
NZ = 8
NT = 8
NG = 16
NST = 16
BR = 32
BC = 448

SOFTMAX_SCALE = 0.0721688
MASK_VALUE = -1e30
MESH = pl.DeviceIdType.MESH
BF16 = jnp.bfloat16
F32 = jnp.float32


def _here():
    s = lax.axis_index("sect")
    g = lax.axis_index("grp")
    t = lax.axis_index("tp")
    yh, z = g // NZ, g % NZ
    yl, x = t // NX, t % NX
    return s, g, t, yh, z, yl, x


def _remote(src, dst, send, recv, dev):
    return pltpu.make_async_remote_copy(
        src_ref=src, dst_ref=dst, send_sem=send, recv_sem=recv, device_id=dev, device_id_type=MESH
    )


def _signal_all(devs):
    barrier = pltpu.get_barrier_semaphore()
    for dev in devs:
        pl.semaphore_signal(barrier, inc=1, device_id=dev, device_id_type=MESH)
    pl.semaphore_wait(barrier, len(devs))


NPIECE = 16


def _layer_kernel(
    own_ref,
    oproj_ref,
    res_ref,
    wg_ref,
    wu_ref,
    wd_ref,
    ids_ref,
    wts_ref,
    out_ref,
    gbuf,
    obuf,
    wbuf,
    wdraw,
    wdbuf,
    resbuf,
    wcol,
    part,
    rbuf,
    mine,
    rows,
    hacc,
    hid,
    tsend,
    pbuf,
    acc,
    ring,
    ybuf,
    fbuf,
    wsem,
    hsend,
    hrecv,
    asend,
    bsend,
    brecv,
    ssend,
    srecv,
    ysend,
    yrecv,
    rsend,
    rrecv,
    psend,
    precv,
    cpsend,
    cprecv,
    crsend,
    crrecv,
    cysend,
    cyrecv,
    cfsend,
    cfrecv,
):
    s, g, t, yh, z, yl, x = _here()
    y = yh * 2 + yl
    d = s * NT + t
    oh = 1 - yh

    def st_dev(e):
        return {"sect": e // NT, "tp": e % NT}

    def y_dev(e):
        return {"grp": (e // 2) * NZ + z, "tp": (e % 2) * NX + x}

    def z_dev(e):
        return {"grp": yh * NZ + e}

    def x_dev(e):
        return {"tp": yl * NX + e}

    partner = {"sect": 1 - s}
    zr, zl = (z + 1) % NZ, (z + NZ - 1) % NZ
    xr, xl = (x + 1) % NX, (x + NX - 1) % NX
    xo = (x + 2) % NX

    loads = [
        pltpu.make_async_copy(wg_ref, wbuf.at[:, pl.ds(0, 128)], wsem.at[0]),
        pltpu.make_async_copy(wu_ref, wbuf.at[:, pl.ds(128, 128)], wsem.at[1]),
        pltpu.make_async_copy(wd_ref, wdraw, wsem.at[2]),
    ]
    for c in loads:
        c.start()

    _signal_all(
        [st_dev((d + o) % NST) for o in range(1, NST)]
        + [z_dev((z + o) % NZ) for o in range(1, NZ)]
        + [y_dev((y + o) % NY) for o in range(1, NY)]
    )

    sent = []

    def start(c):
        c.start()
        sent.append(c)

    def landed(ref, sem):
        _remote(ref, ref, asend.at[0], sem, partner).wait_recv()


    def hop(src, slot, q, way):
        start(
            _remote(
                src, gbuf.at[slot, q], hsend.at[slot, way, q], hrecv.at[slot, q], (z_dev(zr), z_dev(zl))[way]
            )
        )

    for q in range(2):
        h = own_ref.at[q]
        start(_remote(h, gbuf.at[g, q], asend.at[q], hrecv.at[g, q], {"grp": oh * NZ + z}))
        hop(h, g, q, 0)
        hop(h, g, q, 1)

    for c in range(8):
        obuf[pl.ds(128 * c, 128), :] = oproj_ref[:, pl.ds(128 * c, 128)].T
    window = pl.multiple_of((d // 4) * 128, 128)
    resbuf[...] = res_ref[:, pl.ds(window, 128)].T
    pick = (ids_ref[...] == g).astype(F32) * wts_ref[...]
    wcol[...] = jnp.broadcast_to(jnp.sum(pick, axis=0, keepdims=True), (8, NST * BR)).T

    def project(slots, blocks):
        lhs = blocks[0] if len(blocks) == 1 else jnp.concatenate(blocks, axis=0)
        p = jnp.dot(lhs, obuf[...], preferred_element_type=F32).astype(BF16)
        for i, e in enumerate(slots):
            part[e] = p[i * BR : (i + 1) * BR]

            @pl.when(e != d)
            def _():
                _remote(part.at[e], rbuf.at[d], bsend.at[e], brecv.at[d], st_dev(e)).start()

    def block(slot):
        return gbuf[slot].reshape(BR, gbuf.shape[3])

    half = NZ // 2

    def arrive(side, k):
        plane = (yh, oh)[side] * NZ
        if k == 0:
            slot = plane + z
            for q in range(2):
                landed(gbuf.at[slot, q], hrecv.at[slot, q])
                hop(gbuf.at[slot, q], slot, q, 0)
                hop(gbuf.at[slot, q], slot, q, 1)
            return [slot]
        slots = []
        for q in range(2):
            for way in range(2):
                reach = half if way == side else half - 1
                if k > reach:
                    continue
                slot = plane + ((z + NZ - k) % NZ if way == 0 else (z + k) % NZ)
                landed(gbuf.at[slot, q], hrecv.at[slot, q])
                if k < reach:
                    hop(gbuf.at[slot, q], slot, q, way)
                if q == 0:
                    slots.append(slot)
        return slots

    project([g], [own_ref[...].reshape(BR, gbuf.shape[3])])
    for side, k in ((0, 1), (0, 2), (1, 0), (0, 3), (1, 1), (0, 4), (1, 2), (1, 3), (1, 4)):
        slots = arrive(side, k)
        project(slots, [block(e) for e in slots])

    for c in loads:
        c.wait()
    for i in range(8):
        v = wdraw[:, pl.ds(2 * BC * i, 2 * BC)]
        wdbuf[2 * i] = v[:, :BC]
        wdbuf[2 * i + 1] = v[:, BC:]

    base = pl.multiple_of((d % 4) * BR, BR)
    total = resbuf[pl.ds(base, BR), :].astype(F32) + part[d].astype(F32)
    for o in range(1, NST):
        e = (d + NST - o) % NST
        landed(rbuf.at[e], brecv.at[e])
        total = total + rbuf[e].astype(F32)
    mine[...] = total.astype(BF16)
    rows[yh, z, s, t] = total.astype(BF16)
    hacc[...] = jnp.zeros_like(hacc)

    def weights(hh, zz):
        return wbuf[pl.ds(pl.multiple_of((hh * NZ + zz) * BC, BC), BC), :]

    def use_plane(k):
        count = 2 if k in (0, half) else 4

        def step(i, carry):
            hh = i % 2
            zz = (z + (i // 2) * 2 * k + NZ - k) % NZ
            a = rows[hh, zz, 1].reshape(8 * BR, BC)
            p = jnp.dot(a, weights(hh, zz), preferred_element_type=F32)
            hacc[1] += p.reshape(8, BR, 256)
            return carry

        lax.fori_loop(0, count, step, 0)

    def use_group(xx):
        def step(i, carry):
            hh = i // NZ
            zz = i % NZ
            a = jnp.concatenate([rows[hh, zz, 0, xx], rows[hh, zz, 0, NX + xx]], axis=0)
            return carry + jnp.dot(a, weights(hh, zz), preferred_element_type=F32)

        p = lax.fori_loop(0, NG, step, jnp.zeros((2 * BR, 256), F32))
        hacc[0, xx] = p[:BR]
        hacc[0, NX + xx] = p[BR:]

    order = (0, 3, 1, 2)

    @pl.when(s == 0)
    def _():
        def piece(xx, yy):
            return rows.at[yy // 2, :, 0, (yy % 2) * NX + xx]

        mark = len(sent)
        b = rows.at[yh, z, 0, t]
        for o in range(1, NZ):
            start(_remote(b, b, ssend.at[o], srecv.at[z], z_dev((z + o) % NZ)))
        for o in range(1, NZ):
            e = (z + NZ - o) % NZ
            landed(rows.at[yh, e, 0, t], srecv.at[e])

        def to_partner(p, i):
            start(_remote(p, p, psend.at[i], precv.at[i], partner))

        def other(k):
            if k in (0, half):
                for h in range(2):
                    landed(rows.at[h, (z + k) % NZ, 1], precv.at[h if k == 0 else 14 + h])
            else:
                for h in range(2):
                    landed(rows.at[h, (z + NZ - k) % NZ, 1], precv.at[4 * k - 2 + h])
                    landed(rows.at[h, (z + k) % NZ, 1], precv.at[4 * k + h])
            use_plane(k)

        for o in order[1:]:
            p = piece(x, y)
            start(_remote(p, p, ysend.at[o], yrecv.at[o], y_dev((y + o) % NY)))
        for j, o in enumerate(order):
            p = piece(x, (y + NY - o) % NY)
            if o:
                landed(p, yrecv.at[o])
            start(_remote(p, p, rsend.at[0, j], rrecv.at[0, j], x_dev(xr)))
            start(_remote(p, p, rsend.at[1, j], rrecv.at[1, j], x_dev(xl)))
            to_partner(p, j)
        use_group(x)
        for j, o in enumerate(order):
            yy = (y + NY - o) % NY
            p = piece(xl, yy)
            landed(p, rrecv.at[0, j])
            if j % 2 == 0:
                start(_remote(p, p, rsend.at[2, j], rrecv.at[2, j], x_dev(xr)))
            to_partner(p, 4 + j)
            p = piece(xr, yy)
            landed(p, rrecv.at[1, j])
            if j % 2 == 1:
                start(_remote(p, p, rsend.at[2, j], rrecv.at[2, j], x_dev(xl)))
            to_partner(p, 8 + j)
            if j == 1:
                other(0)
        use_group(xl)
        use_group(xr)
        other(1)
        for j, o in enumerate(order):
            p = piece(xo, (y + NY - o) % NY)
            landed(p, rrecv.at[2, j])
            to_partner(p, 12 + j)
        use_group(xo)
        for k in range(2, half + 1):
            other(k)
        for c in sent[mark:]:
            c.wait_send()
        del sent[mark:]

    @pl.when(s == 1)
    def _():
        def piece(zz, hh):
            return rows.at[hh, zz, 1]

        mark = len(sent)
        b = rows.at[yh, z, 1, t]
        for o in range(1, NX):
            start(_remote(b, b, ssend.at[o], srecv.at[o], x_dev((x + o) % NX)))
        for o in range(1, NX):
            e = (x + NX - o) % NX
            landed(rows.at[yh, z, 1, yl * NX + e], srecv.at[o])

        def quad(yy):
            return rows.at[yy // 2, z, 1, pl.ds((yy % 2) * NX, NX)]

        for o in range(1, NY):
            p = quad(y)
            start(_remote(p, p, ysend.at[o], yrecv.at[o], y_dev((y + o) % NY)))
        for o in range(1, NY):
            landed(quad((y + NY - o) % NY), yrecv.at[o])

        def to_partner(p, i):
            start(_remote(p, p, psend.at[i], precv.at[i], partner))

        def other(i, xx):
            for j, o in enumerate(order):
                yy = (y + NY - o) % NY
                landed(rows.at[yy // 2, :, 0, (yy % 2) * NX + xx], precv.at[4 * i + j])
            use_group(xx)

        for h in range(2):
            p = piece(z, h)
            start(_remote(p, p, rsend.at[0, h], rrecv.at[0, h], z_dev(zr)))
            start(_remote(p, p, rsend.at[1, h], rrecv.at[1, h], z_dev(zl)))
            to_partner(p, h)
        use_plane(0)
        for k in range(1, half):
            for h in range(2):
                p = piece((z + NZ - k) % NZ, h)
                landed(p, rrecv.at[0, 2 * (k - 1) + h])
                if k < half - 1 or h == 0:
                    start(_remote(p, p, rsend.at[0, 2 * k + h], rrecv.at[0, 2 * k + h], z_dev(zr)))
                to_partner(p, 4 * k - 2 + h)
                p = piece((z + k) % NZ, h)
                landed(p, rrecv.at[1, 2 * (k - 1) + h])
                if k < half - 1 or h == 1:
                    start(_remote(p, p, rsend.at[1, 2 * k + h], rrecv.at[1, 2 * k + h], z_dev(zl)))
                to_partner(p, 4 * k + h)
            use_plane(k)
            if k == 1:
                other(0, x)
            if k == 3:
                other(1, xl)
                other(2, xr)
        for h in range(2):
            p = piece((z + half) % NZ, h)
            landed(p, rrecv.at[h, 2 * (half - 1) + h])
            to_partner(p, 14 + h)
        use_plane(half)
        other(3, xo)
        for c in sent[mark:]:
            c.wait_send()
        del sent[mark:]

    gate = hacc[:, :, :, :128].reshape(NST * BR, 128)
    up = hacc[:, :, :, 128:].reshape(NST * BR, 128)
    weight = wcol[:, 0:1]
    hid[...] = (weight * (gate / (1.0 + jnp.exp(-gate))) * up).astype(BF16).reshape(2, NT, BR, 128)

    def down_plane(dst, sec, zz, hh):
        a = hid[sec].reshape(NT * BR, 128)
        p = jnp.dot(a, wdbuf[hh * NZ + zz], preferred_element_type=F32)
        dst[hh, zz] = p.astype(BF16).reshape(NT, BR, BC)

    def down_group(dst, sec, xx):
        a = jnp.concatenate([hid[sec, xx], hid[sec, NX + xx]], axis=0)

        def step(i, carry):
            p = jnp.dot(a, wdbuf[i], preferred_element_type=F32).astype(BF16)
            dst[i // NZ, i % NZ, xx] = p[:BR]
            dst[i // NZ, i % NZ, NX + xx] = p[BR:]
            return carry

        lax.fori_loop(0, NG, step, 0)

    def add(dst, srcs, n=8):
        def step(i, carry):
            v = dst[i].astype(F32)
            for r in srcs:
                v = v + r[i].astype(F32)
            dst[i] = v.astype(BF16)
            return carry

        lax.fori_loop(0, n, step, 0)

    def finish(refs):
        tot = refs[0][...].astype(F32)
        for r in refs[1:]:
            tot = tot + r[...].astype(F32)
        out_ref[...] = (mine[...].astype(F32) + tot).astype(BF16)

    xs = (xo, xr, xl, x)
    zs = [(z + half) % NZ]
    for k in range(half - 1, 0, -1):
        zs += [(z + k) % NZ, (z + NZ - k) % NZ]
    zs.append(z)
    ys = ((y + 2) % NY, (y + 1) % NY, (y + NY - 1) % NY, y)

    @pl.when(s == 0)
    def _():
        mark = len(sent)

        def give(i):
            for h in range(2):
                down_plane(tsend, 1, zs[i], h)
                n = 2 * i + h
                start(_remote(tsend.at[h, zs[i]], pbuf.at[h, zs[i]], cpsend.at[n], cprecv.at[n], partner))

        def at(ref, i, j):
            yy = ys[j]
            return ref.at[yy // 2, :, (yy % 2) * NX + xs[i]]

        def take(i, j, more=()):
            landed(at(pbuf, i, j), cprecv.at[4 * i + j])
            add(at(acc, i, j), [at(pbuf, i, j)] + list(more))

        right, left = x_dev(xr), x_dev(xl)
        give(0)
        down_group(acc, 0, xs[0])
        give(1)
        for j in range(4):
            take(0, j)
            start(_remote(at(acc, 0, j), ring.at[j], crsend.at[j], crrecv.at[j], right if j % 2 == 0 else left))
        down_group(acc, 0, xs[1])
        give(2)
        down_group(acc, 0, xs[2])
        give(3)
        for j in range(4):
            for i, way, dev in ((1, 0, right), (2, 1, left)):
                if j % 2 == way:
                    landed(ring.at[j], crrecv.at[j])
                    take(i, j, [ring.at[j]])
                else:
                    take(i, j)
                k = 4 + 4 * way + j
                start(_remote(at(acc, i, j), ring.at[k], crsend.at[k], crrecv.at[k], dev))
            give(4 + j)
        down_group(acc, 0, xs[3])
        for j in range(4):
            landed(ring.at[4 + j], crrecv.at[4 + j])
            landed(ring.at[8 + j], crrecv.at[8 + j])
            take(3, j, [ring.at[4 + j], ring.at[8 + j]])
            if j < 3:
                o = (2, 1, 3)[j]
                start(_remote(at(acc, 3, j), ybuf.at[o], cysend.at[o], cyrecv.at[o], y_dev(ys[j])))
        for o in (2, 1, 3):
            landed(ybuf.at[o], cyrecv.at[o])
        add(at(acc, 3, 3), [ybuf.at[o] for o in (2, 1, 3)])
        for o in range(1, NZ):
            e = (z + o) % NZ
            start(_remote(acc.at[yh, e, t], fbuf.at[o], cfsend.at[o], cfrecv.at[o], z_dev(e)))
        for o in range(1, NZ):
            landed(fbuf.at[o], cfrecv.at[o])
        finish([acc.at[yh, z, t]] + [fbuf.at[o] for o in range(1, NZ)])
        for c in sent[mark:]:
            c.wait_send()
        del sent[mark:]

    @pl.when(s == 1)
    def _():
        mark = len(sent)

        def give(i):
            down_group(tsend, 0, xs[i])
            for j, yy in enumerate(ys):
                tt = (yy % 2) * NX + xs[i]
                n = 4 * i + j
                start(
                    _remote(tsend.at[yy // 2, :, tt], pbuf.at[yy // 2, :, tt], cpsend.at[n], cprecv.at[n], partner)
                )

        def have(i):
            for h in range(2):
                down_plane(acc, 1, zs[i], h)

        def take(i, h, more=()):
            landed(pbuf.at[h, zs[i]], cprecv.at[2 * i + h])
            add(acc.at[h, zs[i]], [pbuf.at[h, zs[i]]] + list(more))

        right, left = z_dev(zr), z_dev(zl)
        give(0)
        have(0)
        for h in range(2):
            take(0, h)
            start(_remote(acc.at[h, zs[0]], ring.at[h], crsend.at[h], crrecv.at[h], (right, left)[h]))
        give(1)
        have(1)
        have(2)
        give(2)
        for k in range(1, half):
            for h in range(2):
                for way, dev in ((0, right), (1, left)):
                    i = 2 * k - 1 + way
                    prev = None
                    if k == 1:
                        if h == way:
                            prev = h
                    else:
                        prev = 2 + 4 * (k - 2) + 2 * way + h
                    if prev is None:
                        take(i, h)
                    else:
                        landed(ring.at[prev], crrecv.at[prev])
                        take(i, h, [ring.at[prev]])
                    q = 2 + 4 * (k - 1) + 2 * way + h
                    start(_remote(acc.at[h, zs[i]], ring.at[q], crsend.at[q], crrecv.at[q], dev))
            if k == 1:
                give(3)
            have(2 * k + 1)
            if k < half - 1:
                have(2 * k + 2)
        for h in range(2):
            q = 2 + 4 * (half - 2) + h
            landed(ring.at[q], crrecv.at[q])
            landed(ring.at[q + 2], crrecv.at[q + 2])
            take(7, h, [ring.at[q], ring.at[q + 2]])

        def quad(yy):
            return acc.at[yy // 2, z, pl.ds((yy % 2) * NX, NX)]

        def qbuf(o):
            return ybuf.at[o, pl.ds(0, NX)]

        for o in (2, 1, 3):
            e = (y + o) % NY
            start(_remote(quad(e), qbuf(o), cysend.at[o], cyrecv.at[o], y_dev(e)))
        for o in (2, 1, 3):
            landed(qbuf(o), cyrecv.at[o])
        add(quad(y), [qbuf(o) for o in (2, 1, 3)], NX)
        for o in range(1, NX):
            e = (x + o) % NX
            start(_remote(acc.at[yh, z, yl * NX + e], fbuf.at[o], cfsend.at[o], cfrecv.at[o], x_dev(e)))
        for o in range(1, NX):
            landed(fbuf.at[o], cfrecv.at[o])
        finish([acc.at[yh, z, t]] + [fbuf.at[o] for o in range(1, NX)])
        for c in sent[mark:]:
            c.wait_send()
        del sent[mark:]

    for o in range(1, NST):
        e = (d + o) % NST
        _remote(part.at[e], rbuf.at[d], bsend.at[e], brecv.at[d], st_dev(e)).wait_send()
    for c in sent:
        c.wait_send()


def layer_rest(heads, out_proj, residual, w_gate, w_up, w_down, route_ids, route_weights):
    vmem = pl.BlockSpec(memory_space=pltpu.VMEM)
    hbm = pl.BlockSpec(memory_space=pl.ANY)
    dma = pltpu.SemaphoreType.DMA
    depth = heads.shape[1]
    scratch = [
        pltpu.VMEM((NG, 2, BR // 2, depth), BF16),
        pltpu.VMEM((depth, BC), BF16),
        pltpu.VMEM(w_gate.shape[:1] + (256,), BF16),
        pltpu.VMEM(w_down.shape, BF16),
        pltpu.VMEM((NG, 128, BC), BF16),
        pltpu.VMEM((128, BC), BF16),
        pltpu.VMEM((NST * BR, 8), F32),
        pltpu.VMEM((NST, BR, BC), BF16),
        pltpu.VMEM((NST, BR, BC), BF16),
        pltpu.VMEM((BR, BC), BF16),
        pltpu.VMEM((2, NZ, 2, NT, BR, BC), BF16),
        pltpu.VMEM((2, NT, BR, 256), F32),
        pltpu.VMEM((2, NT, BR, 128), BF16),
        pltpu.VMEM((2, NZ, NT, BR, BC), BF16),
        pltpu.VMEM((2, NZ, NT, BR, BC), BF16),
        pltpu.VMEM((2, NZ, NT, BR, BC), BF16),
        pltpu.VMEM((16, 8, BR, BC), BF16),
        pltpu.VMEM((4, 8, BR, BC), BF16),
        pltpu.VMEM((8, BR, BC), BF16),
        dma((3,)),
        dma((NG, 2, 2)),
        dma((NG, 2)),
        dma((2,)),
        dma((NST,)),
        dma((NST,)),
        dma((NZ,)),
        dma((NZ,)),
        dma((NY,)),
        dma((NY,)),
        dma((3, NZ)),
        dma((3, NZ)),
        dma((16,)),
        dma((16,)),
        dma((16,)),
        dma((16,)),
        dma((16,)),
        dma((16,)),
        dma((4,)),
        dma((4,)),
        dma((8,)),
        dma((8,)),
    ]
    return pl.pallas_call(
        _layer_kernel,
        out_shape=jax.ShapeDtypeStruct((BR, BC), BF16),
        in_specs=[vmem, vmem, vmem, hbm, hbm, hbm, vmem, vmem],
        out_specs=vmem,
        scratch_shapes=scratch,
        compiler_params=pltpu.CompilerParams(
            collective_id=0, has_side_effects=True, vmem_limit_bytes=60 * 1024 * 1024
        ),
        name="layer_rest",
    )(
        heads.reshape(2, BR // 2, depth),
        out_proj.T,
        residual.T,
        w_gate,
        w_up,
        w_down,
        route_ids.T,
        route_weights.T,
    )


def on_device(
    queries,
    latent_cache,
    cache_len,
    value_up,
    out_proj,
    residual,
    w_gate,
    w_up,
    w_down,
    route_ids,
    route_weights,
):
    local_rows = queries.shape[0]
    local_heads = queries.shape[1]
    scores = (
        jnp.einsum("rhk,rlk->rhl", queries, latent_cache, preferred_element_type=F32) * SOFTMAX_SCALE
    )
    positions = jnp.arange(latent_cache.shape[1], dtype=jnp.int32)
    in_range = positions[None, None, :] < cache_len[:, None, None]
    masked = jnp.where(in_range, scores, MASK_VALUE)
    row_max = jnp.max(masked, axis=2, keepdims=True)
    exp_scores = jnp.where(in_range, jnp.exp(masked - row_max), 0.0)
    probs = (exp_scores / jnp.sum(exp_scores, axis=2, keepdims=True)).astype(BF16)
    latent_out = jnp.einsum(
        "rhl,rlc->rhc", probs, latent_cache[:, :, :LAT], preferred_element_type=F32
    ).astype(BF16)
    heads_out = jnp.einsum("rhc,hcv->rhv", latent_out, value_up, preferred_element_type=F32)
    heads_out = heads_out.astype(BF16).reshape(local_rows, local_heads * VDIM)
    return layer_rest(
        heads_out, out_proj, residual, w_gate[0], w_up[0], w_down[0], route_ids, route_weights
    )


def solution(mesh):
    return jax.shard_map(
        on_device,
        mesh=mesh,
        in_specs=(
            P("grp", ("sect", "tp"), None),
            P("grp", None, None),
            P("grp"),
            P(("sect", "tp"), None, None),
            P(("sect", "tp"), "grp"),
            P(None, "grp"),
            P("grp", None, ("sect", "tp")),
            P("grp", None, ("sect", "tp")),
            P("grp", ("sect", "tp"), None),
            P(),
            P(),
        ),
        out_specs=P(("sect", "tp"), "grp"),
        check_vma=False,
    )
```

```python
import jax
import jax.numpy as jnp
from jax import lax
from jax.experimental import pallas as pl
from jax.experimental.pallas import tpu as pltpu
from jax.sharding import PartitionSpec as P

LAT = 512
VDIM = 128
NX = 4
NY = 4
NZ = 8
NT = 8
NG = 16
NST = 16
BR = 32
BC = 448

SOFTMAX_SCALE = 0.0721688
MASK_VALUE = -1e30
MESH = pl.DeviceIdType.MESH
BF16 = jnp.bfloat16
F32 = jnp.float32


def _here():
    s = lax.axis_index("sect")
    g = lax.axis_index("grp")
    t = lax.axis_index("tp")
    yh, z = g // NZ, g % NZ
    yl, x = t // NX, t % NX
    return s, g, t, yh, z, yl, x


def _remote(src, dst, send, recv, dev):
    return pltpu.make_async_remote_copy(
        src_ref=src, dst_ref=dst, send_sem=send, recv_sem=recv, device_id=dev, device_id_type=MESH
    )


def _signal_all(devs):
    for dev in devs:
        pl.semaphore_signal(pltpu.get_barrier_semaphore(), inc=1, device_id=dev, device_id_type=MESH)
    return len(devs)


def _layer_kernel(
    len_ref,
    q_ref,
    cache_ref,
    vup_ref,
    oproj_ref,
    res_ref,
    wg_ref,
    wu_ref,
    wd_ref,
    ids_ref,
    wts_ref,
    out_ref,
    cbuf,
    vbuf,
    sbuf,
    lbuf,
    own_ref,
    gbuf,
    obuf,
    wbuf,
    wdraw,
    wdbuf,
    resbuf,
    wcol,
    part,
    rbuf,
    mine,
    rows,
    hacc,
    hid,
    tsend,
    pbuf,
    acc,
    ring,
    ybuf,
    fbuf,
    csem,
    wsem,
    hsend,
    hrecv,
    asend,
    bsend,
    brecv,
    ssend,
    srecv,
    ysend,
    yrecv,
    rsend,
    rrecv,
    psend,
    precv,
    cpsend,
    cprecv,
    crsend,
    crrecv,
    cysend,
    cyrecv,
    cfsend,
    cfrecv,
):
    s, g, t, yh, z, yl, x = _here()
    y = yh * 2 + yl
    d = s * NT + t
    oh = 1 - yh

    def st_dev(e):
        return {"sect": e // NT, "tp": e % NT}

    def y_dev(e):
        return {"grp": (e // 2) * NZ + z, "tp": (e % 2) * NX + x}

    def z_dev(e):
        return {"grp": yh * NZ + e}

    def x_dev(e):
        return {"tp": yl * NX + e}

    def xy_dev(ex, ey):
        return {"grp": (ey // 2) * NZ + z, "tp": (ey % 2) * NX + ex}

    partner = {"sect": 1 - s}
    zr, zl = (z + 1) % NZ, (z + NZ - 1) % NZ
    xr, xl = (x + 1) % NX, (x + NX - 1) % NX
    xo = (x + 2) % NX

    chunk = BR // 2
    fetch = [
        pltpu.make_async_copy(
            cache_ref.at[pl.ds(chunk * q, chunk)], cbuf.at[pl.ds(chunk * q, chunk)], csem.at[q]
        )
        for q in range(2)
    ]
    fetch.append(pltpu.make_async_copy(vup_ref, vbuf, csem.at[2]))
    for c in (fetch[0], fetch[2], fetch[1]):
        c.start()
    loads = [
        pltpu.make_async_copy(wg_ref, wbuf.at[:, pl.ds(0, 128)], wsem.at[0]),
        pltpu.make_async_copy(wu_ref, wbuf.at[:, pl.ds(128, 128)], wsem.at[1]),
        pltpu.make_async_copy(wd_ref, wdraw, wsem.at[2]),
    ]
    for c in loads:
        c.start()

    expected = _signal_all(
        [st_dev((d + o) % NST) for o in range(1, NST)]
        + [z_dev((z + o) % NZ) for o in range(1, NZ)]
        + [y_dev((y + o) % NY) for o in range(1, NY)]
        + [{"grp": oh * NZ + z, "tp": (t + o) % NT} for o in range(1, NT)]
    )

    sent = []

    def start(c):
        c.start()
        sent.append(c)

    def landed(ref, sem):
        _remote(ref, ref, asend.at[0], sem, partner).wait_recv()


    steps = [z_dev((z + o) % NZ) for o in (1, NZ - 1, 2, NZ - 2)] + [{"grp": oh * NZ + z}]

    def hop(src, slot, q, way):
        start(_remote(src, gbuf.at[slot, q], hsend.at[slot, q, way], hrecv.at[slot, q], steps[way]))

    def attend(q):
        fetch[q].wait()
        heads = q_ref.shape[1]
        shape = (heads, cbuf.shape[2])
        positions = lax.broadcasted_iota(jnp.int32, shape, 1)
        for i in range(chunk):
            r = chunk * q + i
            score = jnp.dot(q_ref[r], cbuf[r], preferred_element_type=F32) * SOFTMAX_SCALE
            sbuf[i] = jnp.where(positions < len_ref[r], score, MASK_VALUE)
        score = sbuf[...]
        top = jnp.max(score, axis=2, keepdims=True)
        e = jnp.where(score > 0.5 * MASK_VALUE, jnp.exp(score - top), 0.0)
        sbuf[...] = e / jnp.sum(e, axis=2, keepdims=True)
        for i in range(chunk):
            r = chunk * q + i
            latent = lax.dot_general(
                sbuf[i].astype(BF16), cbuf[r, :LAT], (((1,), (1,)), ((), ())), preferred_element_type=F32
            )
            lbuf[i] = latent.astype(BF16).astype(F32)
        if q == 0:
            fetch[2].wait()
        for h in range(heads):
            value = jnp.dot(lbuf[:, h, :].astype(BF16), vbuf[h], preferred_element_type=F32)
            own_ref[q, :, VDIM * h : VDIM * (h + 1)] = value.astype(BF16)

    for q in range(2):
        attend(q)
        if q == 0:
            pl.semaphore_wait(pltpu.get_barrier_semaphore(), expected)
        for way in (4, 2, 3, 0, 1):
            hop(own_ref.at[q], g, q, way)

    for c in range(8):
        obuf[pl.ds(128 * c, 128), :] = oproj_ref[:, pl.ds(128 * c, 128)].T
    window = pl.multiple_of((d // 4) * 128, 128)
    resbuf[...] = res_ref[:, pl.ds(window, 128)].T
    pick = (ids_ref[...] == g).astype(F32) * wts_ref[...]
    wcol[...] = jnp.broadcast_to(jnp.sum(pick, axis=0, keepdims=True), (8, NST * BR)).T

    def project(slots, blocks):
        lhs = blocks[0] if len(blocks) == 1 else jnp.concatenate(blocks, axis=0)
        p = jnp.dot(lhs, obuf[...], preferred_element_type=F32).astype(BF16)
        for i, e in enumerate(slots):
            part[e] = p[i * BR : (i + 1) * BR]

            @pl.when(e != d)
            def _():
                _remote(part.at[e], rbuf.at[d], bsend.at[e], brecv.at[d], st_dev(e)).start()

    def block(slot):
        return gbuf[slot].reshape(BR, gbuf.shape[3])

    half = NZ // 2

    def arrive(side, k):
        slots = []
        for q in range(2):
            for way in range(1 if k in (0, half) else 2):
                slot = (yh, oh)[side] * NZ + (z + NZ - k if way == 0 else z + k) % NZ
                landed(gbuf.at[slot, q], hrecv.at[slot, q])
                if side == 0 and k == 2:
                    hop(gbuf.at[slot, q], slot, q, way)
                    if q == way:
                        hop(gbuf.at[slot, q], slot, q, 2 + way)
                if side == 0 and k > 2:
                    hop(gbuf.at[slot, q], slot, q, 4)
                if side == 1 and k == 0:
                    for w in (2, 3, 0, 1):
                        hop(gbuf.at[slot, q], slot, q, w)
                if q == 0:
                    slots.append(slot)
        return slots

    held, blocks = [g], [own_ref[...].reshape(BR, gbuf.shape[3])]
    for side, k, now in (
        (0, 1, 0),
        (0, 2, 0),
        (1, 0, 1),
        (0, 3, 0),
        (0, 4, 1),
        (1, 1, 0),
        (1, 2, 1),
        (1, 3, 1),
        (1, 4, 1),
    ):
        slots = arrive(side, k)
        held += slots
        blocks += [block(e) for e in slots]
        if now:
            project(held, blocks)
            held, blocks = [], []

    for c in loads:
        c.wait()
    for i in range(8):
        v = wdraw[:, pl.ds(2 * BC * i, 2 * BC)]
        wdbuf[2 * i] = v[:, :BC]
        wdbuf[2 * i + 1] = v[:, BC:]

    base = pl.multiple_of((d % 4) * BR, BR)
    total = resbuf[pl.ds(base, BR), :].astype(F32) + part[d].astype(F32)
    for o in range(1, NST):
        e = (d + NST - o) % NST
        landed(rbuf.at[e], brecv.at[e])
        total = total + rbuf[e].astype(F32)
    mine[...] = total.astype(BF16)
    rows[yh, z, s, t] = total.astype(BF16)
    hacc[...] = jnp.zeros_like(hacc)

    def weights(hh, zz):
        return wbuf[pl.ds(pl.multiple_of((hh * NZ + zz) * BC, BC), BC), :]

    def use_plane(k):
        count = 2 if k in (0, half) else 4

        def step(i, carry):
            hh = i % 2
            zz = (z + (i // 2) * 2 * k + NZ - k) % NZ
            a = rows[hh, zz, 1].reshape(8 * BR, BC)
            p = jnp.dot(a, weights(hh, zz), preferred_element_type=F32)
            hacc[1] += p.reshape(8, BR, 256)
            return carry

        lax.fori_loop(0, count, step, 0)

    def use_group(*xx):
        places = [o + e for e in xx for o in (0, NX)]

        def step(i, carry):
            hh = i // NZ
            zz = i % NZ
            a = jnp.concatenate([rows[hh, zz, 0, e] for e in places], axis=0)
            return carry + jnp.dot(a, weights(hh, zz), preferred_element_type=F32)

        p = lax.fori_loop(0, NG, step, jnp.zeros((len(places) * BR, 256), F32))
        for i, e in enumerate(places):
            hacc[0, e] = p[i * BR : (i + 1) * BR]

    ymine = (y, (y + NY - 1) % NY, (y + 1) % NY, (y + 2) % NY)

    def quad_of(zz, yy):
        return rows.at[yy // 2, zz, 1, pl.ds((yy % 2) * NX, NX)]

    def qid(k, way, j):
        return j if k == 0 else 8 * k - 4 + 4 * way + j

    @pl.when(s == 0)
    def _():
        def piece(xx, yy):
            return rows.at[yy // 2, :, 0, (yy % 2) * NX + xx]

        mark = len(sent)
        b = rows.at[yh, z, 0, t]
        for o in range(1, NZ):
            start(_remote(b, b, ssend.at[o], srecv.at[z], z_dev((z + o) % NZ)))
        for o in range(1, NZ):
            e = (z + NZ - o) % NZ
            landed(rows.at[yh, e, 0, t], srecv.at[e])

        def to_partner(p, i):
            start(_remote(p, p, psend.at[i], precv.at[i], partner))

        def other(k):
            for j in range(4):
                for way in range(1 if k in (0, half) else 2):
                    landed(quad_of((z + NZ - k if way == 0 else z + k) % NZ, ymine[j]), precv.at[qid(k, way, j)])
            use_plane(k)

        yr, yl_ = y_dev((y + 1) % NY), y_dev((y + NY - 1) % NY)
        p = piece(x, y)
        start(_remote(p, p, ysend.at[0], yrecv.at[0], yr))
        start(_remote(p, p, ysend.at[1], yrecv.at[1], yl_))

        def out(j):
            q = piece(x, ymine[j])
            start(_remote(q, q, rsend.at[0, j], rrecv.at[0, j], x_dev(xr)))
            start(_remote(q, q, rsend.at[1, j], rrecv.at[1, j], x_dev(xl)))
            to_partner(q, j)

        def halfof(w):
            yy = ymine[(1, 2)[w]]
            return rows.at[yy // 2, pl.ds(4 * w, 4), 0, (yy % 2) * NX + x]

        def halfin(w):
            yy = ymine[3]
            return rows.at[yy // 2, pl.ds(4 * w, 4), 0, (yy % 2) * NX + x]

        def ring_in(j):
            q = piece(xl, ymine[j])
            landed(q, rrecv.at[0, j])
            if j % 2 == 0:
                start(_remote(q, q, rsend.at[0, 4 + j], rrecv.at[0, 4 + j], x_dev(xr)))
            to_partner(q, 4 + j)
            q = piece(xr, ymine[j])
            landed(q, rrecv.at[1, j])
            if j % 2 == 1:
                start(_remote(q, q, rsend.at[1, 4 + j], rrecv.at[1, 4 + j], x_dev(xl)))
            to_partner(q, 8 + j)

        out(0)
        for w in range(2):
            landed(piece(x, ymine[1 + w]), yrecv.at[w])
            q = halfof(w)
            start(_remote(q, q, ysend.at[2 + w], yrecv.at[2 + w], (yr, yl_)[w]))
            out(1 + w)
        ring_in(0)
        for w in range(2):
            landed(halfin(w), yrecv.at[2 + w])
        out(3)
        use_group(x)
        ring_in(1)
        ring_in(2)
        other(0)
        ring_in(3)
        use_group(xl, xr)
        other(1)
        for j in range(4):
            p = piece(xo, ymine[j])
            landed(p, rrecv.at[j % 2, 4 + j])
            to_partner(p, 12 + j)
        use_group(xo)
        for k in range(2, half + 1):
            other(k)
        for c in sent[mark:]:
            c.wait_send()
        del sent[mark:]

    @pl.when(s == 1)
    def _():
        def piece(zz, hh):
            return rows.at[hh, zz, 1]

        mark = len(sent)
        b = rows.at[yh, z, 1, t]
        for oy in (0, 1, 3, 2):
            for ox in range(NX):
                if oy + ox:
                    n = oy * NX + ox
                    start(_remote(b, b, ssend.at[n], srecv.at[n], xy_dev((x + ox) % NX, (y + oy) % NY)))

        def to_partner(p, i):
            start(_remote(p, p, psend.at[i], precv.at[i], partner))

        def other(i, *xx):
            for e in xx:
                for j in range(4):
                    yy = ymine[j]
                    landed(rows.at[yy // 2, :, 0, (yy % 2) * NX + e], precv.at[4 * i + j])
                i = i + 1
            use_group(*xx)

        def out(j):
            q = quad_of(z, ymine[j])
            start(_remote(q, q, rsend.at[0, j], rrecv.at[0, j], z_dev(zr)))
            start(_remote(q, q, rsend.at[1, j], rrecv.at[1, j], z_dev(zl)))
            to_partner(q, qid(0, 0, j))

        def ring_in(k, j):
            n = 4 * k + j
            for way in range(2):
                if k == half and j % 2 != way:
                    continue
                q = quad_of((z + NZ - k if way == 0 else z + k) % NZ, ymine[j])
                landed(q, rrecv.at[way, n - 4])
                if k < half - 1 or (k == half - 1 and j % 2 == way):
                    start(_remote(q, q, rsend.at[way, n], rrecv.at[way, n], z_dev((zr, zl)[way])))
                to_partner(q, qid(k, 0 if k == half else way, j))

        for j, oy in enumerate((0, 1, 3, 2)):
            yy = ymine[j]
            for ox in range(NX):
                if oy + ox:
                    n = oy * NX + ox
                    landed(rows.at[yy // 2, z, 1, (yy % 2) * NX + (x + NX - ox) % NX], srecv.at[n])
            out(j)
        use_plane(0)
        for k in range(1, half + 1):
            for j in range(4):
                ring_in(k, j)
            if k < half:
                use_plane(k)
            if k == 2:
                other(0, x)
            if k == 3:
                other(1, xl, xr)
        use_plane(half)
        other(3, xo)
        for c in sent[mark:]:
            c.wait_send()
        del sent[mark:]

    gate = hacc[:, :, :, :128].reshape(NST * BR, 128)
    up = hacc[:, :, :, 128:].reshape(NST * BR, 128)
    weight = wcol[:, 0:1]
    hid[...] = (weight * (gate / (1.0 + jnp.exp(-gate))) * up).astype(BF16).reshape(2, NT, BR, 128)

    def down_plane(dst, sec, zz, hh):
        a = hid[sec].reshape(NT * BR, 128)
        p = jnp.dot(a, wdbuf[hh * NZ + zz], preferred_element_type=F32)
        dst[hh, zz] = p.astype(BF16).reshape(NT, BR, BC)

    def down_group(dst, sec, xx):
        a = jnp.concatenate([hid[sec, xx], hid[sec, NX + xx]], axis=0)

        def step(i, carry):
            p = jnp.dot(a, wdbuf[i], preferred_element_type=F32).astype(BF16)
            dst[i // NZ, i % NZ, xx] = p[:BR]
            dst[i // NZ, i % NZ, NX + xx] = p[BR:]
            return carry

        lax.fori_loop(0, NG, step, 0)

    def add(dst, srcs, n=8):
        def step(i, carry):
            v = dst[i].astype(F32)
            for r in srcs:
                v = v + r[i].astype(F32)
            dst[i] = v.astype(BF16)
            return carry

        lax.fori_loop(0, n, step, 0)

    def finish(refs):
        tot = refs[0][...].astype(F32)
        for r in refs[1:]:
            tot = tot + r[...].astype(F32)
        out_ref[...] = (mine[...].astype(F32) + tot).astype(BF16)

    xs = (xo, xr, xl, x)
    zs = [(z + half) % NZ]
    for k in range(half - 1, 0, -1):
        zs += [(z + k) % NZ, (z + NZ - k) % NZ]
    zs.append(z)
    ys = ((y + 2) % NY, (y + 1) % NY, (y + NY - 1) % NY, y)
    yright, yleft = y_dev((y + 1) % NY), y_dev((y + NY - 1) % NY)

    def quad(ref, i, j):
        return ref.at[ys[j] // 2, zs[i], pl.ds((ys[j] % 2) * NX, NX)]

    @pl.when(s == 0)
    def _():
        mark = len(sent)

        def give(i):
            for h in range(2):
                down_plane(tsend, 1, zs[i], h)
            for j in range(4):
                n = 4 * i + j
                start(_remote(quad(tsend, i, j), quad(pbuf, i, j), cpsend.at[n], cprecv.at[n], partner))

        def at(ref, i, j):
            yy = ys[j]
            return ref.at[yy // 2, :, (yy % 2) * NX + xs[i]]

        def take(i, j, more=()):
            landed(at(pbuf, i, j), cprecv.at[4 * i + j])
            add(at(acc, i, j), [at(pbuf, i, j)] + list(more))

        right, left = x_dev(xr), x_dev(xl)
        give(0)
        down_group(acc, 0, xs[0])
        give(1)
        for j in range(4):
            take(0, j)
            start(_remote(at(acc, 0, j), ring.at[j], crsend.at[j], crrecv.at[j], right if j % 2 == 0 else left))
        down_group(acc, 0, xs[1])
        give(2)
        down_group(acc, 0, xs[2])
        give(3)
        for j in range(4):
            for i, way, dev in ((1, 0, right), (2, 1, left)):
                if j % 2 == way:
                    landed(ring.at[j], crrecv.at[j])
                    take(i, j, [ring.at[j]])
                else:
                    take(i, j)
                k = 4 + 4 * way + j
                start(_remote(at(acc, i, j), ring.at[k], crsend.at[k], crrecv.at[k], dev))
            give(4 + j)
        down_group(acc, 0, xs[3])
        for j in range(4):
            landed(ring.at[4 + j], crrecv.at[4 + j])
            landed(ring.at[8 + j], crrecv.at[8 + j])
            take(3, j, [ring.at[4 + j], ring.at[8 + j]])
            yy = ys[j]
            tt = (yy % 2) * NX + x
            if j == 0:
                for w in range(2):
                    part4 = pl.ds(4 * w, 4)
                    start(
                        _remote(
                            acc.at[yy // 2, part4, tt],
                            ybuf.at[0, part4],
                            cysend.at[w],
                            cyrecv.at[w],
                            (yright, yleft)[w],
                        )
                    )
            elif j < 3:
                w = j - 1
                part4 = pl.ds(4 * w, 4)
                landed(ybuf.at[0, part4], cyrecv.at[w])
                add(acc.at[yy // 2, part4, tt], [ybuf.at[0, part4]], 4)
                start(
                    _remote(at(acc, 3, j), ybuf.at[j], cysend.at[1 + j], cyrecv.at[1 + j], (yright, yleft)[w])
                )
        for j in (1, 2):
            landed(ybuf.at[j], cyrecv.at[1 + j])
        add(at(acc, 3, 3), [ybuf.at[1], ybuf.at[2]])
        for o in range(1, NZ):
            e = (z + o) % NZ
            start(_remote(acc.at[yh, e, t], fbuf.at[o], cfsend.at[o], cfrecv.at[o], z_dev(e)))
        for o in range(1, NZ):
            landed(fbuf.at[o], cfrecv.at[o])
        finish([acc.at[yh, z, t]] + [fbuf.at[o] for o in range(1, NZ)])
        for c in sent[mark:]:
            c.wait_send()
        del sent[mark:]

    @pl.when(s == 1)
    def _():
        mark = len(sent)

        def give(i):
            down_group(tsend, 0, xs[i])
            for j, yy in enumerate(ys):
                tt = (yy % 2) * NX + xs[i]
                n = 4 * i + j
                start(
                    _remote(tsend.at[yy // 2, :, tt], pbuf.at[yy // 2, :, tt], cpsend.at[n], cprecv.at[n], partner)
                )

        def have(i):
            for h in range(2):
                down_plane(acc, 1, zs[i], h)

        def take(i, j, more=()):
            landed(quad(pbuf, i, j), cprecv.at[4 * i + j])
            add(quad(acc, i, j), [quad(pbuf, i, j)] + list(more), NX)

        def slot(n):
            return ring.at[n // 2, pl.ds((n % 2) * NX, NX)]

        right, left = z_dev(zr), z_dev(zl)
        give(0)
        have(0)
        for j in range(4):
            take(0, j)
            start(_remote(quad(acc, 0, j), slot(j), crsend.at[j], crrecv.at[j], (right, left)[j % 2]))
        have(1)
        have(2)
        give(1)
        for k in range(1, half):
            for j in range(4):
                for way, dev in ((0, right), (1, left)):
                    i = 2 * k - 1 + way
                    prev = 4 + 8 * (k - 2) + 4 * way + j
                    if k == 1:
                        prev = j if j % 2 == way else None
                    if prev is None:
                        take(i, j)
                    else:
                        landed(slot(prev), crrecv.at[prev])
                        take(i, j, [slot(prev)])
                    q = 4 + 8 * (k - 1) + 4 * way + j
                    start(_remote(quad(acc, i, j), slot(q), crsend.at[q], crrecv.at[q], dev))
            if k == 1:
                give(2)
                give(3)
            have(2 * k + 1)
            if k < half - 1:
                have(2 * k + 2)

        for j in range(4):
            q = 4 + 8 * (half - 2) + j
            landed(slot(q), crrecv.at[q])
            landed(slot(q + 4), crrecv.at[q + 4])
            take(7, j, [slot(q), slot(q + 4)])
            oy = (2, 1, 3, 0)[j]
            for ox in range(NX):
                if oy + ox:
                    n = oy * NX + ox
                    ex = (x + ox) % NX
                    src = acc.at[ys[j] // 2, z, (ys[j] % 2) * NX + ex]
                    start(_remote(src, fbuf.at[n], cfsend.at[n], cfrecv.at[n], xy_dev(ex, ys[j])))
        for n in range(1, NY * NX):
            landed(fbuf.at[n], cfrecv.at[n])
        finish([acc.at[yh, z, t]] + [fbuf.at[n] for n in range(1, NY * NX)])
        for c in sent[mark:]:
            c.wait_send()
        del sent[mark:]

    for o in range(1, NST):
        e = (d + o) % NST
        _remote(part.at[e], rbuf.at[d], bsend.at[e], brecv.at[d], st_dev(e)).wait_send()
    for c in sent:
        c.wait_send()


def layer(queries, latent_cache, cache_len, value_up, out_proj, residual, w_gate, w_up, w_down, route_ids, route_weights):
    vmem = pl.BlockSpec(memory_space=pltpu.VMEM)
    hbm = pl.BlockSpec(memory_space=pl.ANY)
    dma = pltpu.SemaphoreType.DMA
    depth = value_up.shape[0] * VDIM
    scratch = [
        pltpu.VMEM((BR, latent_cache.shape[2], latent_cache.shape[1]), BF16),
        pltpu.VMEM(value_up.shape, BF16),
        pltpu.VMEM((BR // 2, queries.shape[1], latent_cache.shape[1]), F32),
        pltpu.VMEM((BR // 2, queries.shape[1], LAT), F32),
        pltpu.VMEM((2, BR // 2, depth), BF16),
        pltpu.VMEM((NG, 2, BR // 2, depth), BF16),
        pltpu.VMEM((depth, BC), BF16),
        pltpu.VMEM(w_gate.shape[:1] + (256,), BF16),
        pltpu.VMEM(w_down.shape, BF16),
        pltpu.VMEM((NG, 128, BC), BF16),
        pltpu.VMEM((128, BC), BF16),
        pltpu.VMEM((NST * BR, 8), F32),
        pltpu.VMEM((NST, BR, BC), BF16),
        pltpu.VMEM((NST, BR, BC), BF16),
        pltpu.VMEM((BR, BC), BF16),
        pltpu.VMEM((2, NZ, 2, NT, BR, BC), BF16),
        pltpu.VMEM((2, NT, BR, 256), F32),
        pltpu.VMEM((2, NT, BR, 128), BF16),
        pltpu.VMEM((2, NZ, NT, BR, BC), BF16),
        pltpu.VMEM((2, NZ, NT, BR, BC), BF16),
        pltpu.VMEM((2, NZ, NT, BR, BC), BF16),
        pltpu.VMEM((16, 8, BR, BC), BF16),
        pltpu.VMEM((3, 8, BR, BC), BF16),
        pltpu.VMEM((16, BR, BC), BF16),
        dma((3,)),
        dma((3,)),
        dma((NG, 2, 5)),
        dma((NG, 2)),
        dma((1,)),
        dma((NST,)),
        dma((NST,)),
        dma((16,)),
        dma((16,)),
        dma((NY,)),
        dma((NY,)),
        dma((2, 16)),
        dma((2, 16)),
        dma((32,)),
        dma((32,)),
        dma((32,)),
        dma((32,)),
        dma((28,)),
        dma((28,)),
        dma((4,)),
        dma((4,)),
        dma((16,)),
        dma((16,)),
    ]
    return pl.pallas_call(
        _layer_kernel,
        out_shape=jax.ShapeDtypeStruct((BR, BC), BF16),
        in_specs=[pl.BlockSpec(memory_space=pltpu.SMEM), vmem, hbm, hbm, vmem, vmem, hbm, hbm, hbm, vmem, vmem],
        out_specs=vmem,
        scratch_shapes=scratch,
        compiler_params=pltpu.CompilerParams(
            collective_id=0, has_side_effects=True, vmem_limit_bytes=60 * 1024 * 1024
        ),
        name="layer",
    )(
        cache_len,
        queries,
        latent_cache.transpose(0, 2, 1),
        value_up,
        out_proj.T,
        residual.T,
        w_gate,
        w_up,
        w_down,
        route_ids.T,
        route_weights.T,
    )


def on_device(
    queries,
    latent_cache,
    cache_len,
    value_up,
    out_proj,
    residual,
    w_gate,
    w_up,
    w_down,
    route_ids,
    route_weights,
):
    return layer(
        queries,
        latent_cache,
        cache_len,
        value_up,
        out_proj,
        residual,
        w_gate[0],
        w_up[0],
        w_down[0],
        route_ids,
        route_weights,
    )


def solution(mesh):
    return jax.shard_map(
        on_device,
        mesh=mesh,
        in_specs=(
            P("grp", ("sect", "tp"), None),
            P("grp", None, None),
            P("grp"),
            P(("sect", "tp"), None, None),
            P(("sect", "tp"), "grp"),
            P(None, "grp"),
            P("grp", None, ("sect", "tp")),
            P("grp", None, ("sect", "tp")),
            P("grp", ("sect", "tp"), None),
            P(),
            P(),
        ),
        out_specs=P(("sect", "tp"), "grp"),
        check_vma=False,
    )
```

```python
import jax
import jax.numpy as jnp
from jax import lax
from jax.experimental import pallas as pl
from jax.experimental.pallas import tpu as pltpu
from jax.sharding import PartitionSpec as P

LAT = 512
VDIM = 128
NX = 4
NY = 4
NZ = 8
NT = 8
NG = 16
NST = 16
BR = 32
BC = 448
TILE = 16
PACK = 7 * TILE
WIDE = 512

SOFTMAX_SCALE = 0.0721688
MASK_VALUE = -1e30
MESH = pl.DeviceIdType.MESH
BF16 = jnp.bfloat16
F32 = jnp.float32


def _here():
    s = lax.axis_index("sect")
    g = lax.axis_index("grp")
    t = lax.axis_index("tp")
    yh, z = g // NZ, g % NZ
    yl, x = t // NX, t % NX
    return s, g, t, yh, z, yl, x


def _remote(src, dst, send, recv, dev):
    return pltpu.make_async_remote_copy(
        src_ref=src, dst_ref=dst, send_sem=send, recv_sem=recv, device_id=dev, device_id_type=MESH
    )


def _signal_all(devs):
    for dev in devs:
        pl.semaphore_signal(pltpu.get_barrier_semaphore(), inc=1, device_id=dev, device_id_type=MESH)
    return len(devs)


def _layer_kernel(
    len_ref,
    q_ref,
    cache_ref,
    vup_ref,
    oproj_ref,
    res_ref,
    wg_ref,
    wu_ref,
    wd_ref,
    ids_ref,
    wts_ref,
    out_ref,
    cbuf,
    vbuf,
    sbuf,
    lbuf,
    own_ref,
    gbuf,
    obuf,
    wbuf,
    wdraw,
    wdbuf,
    resbuf,
    wcol,
    part,
    rbuf,
    mine,
    rows,
    hacc,
    hid,
    tsend,
    pbuf,
    acc,
    ring,
    ybuf,
    fbuf,
    tmp,
    csem,
    wsem,
    hsend,
    hrecv,
    asend,
    bsend,
    brecv,
    ssend,
    srecv,
    ysend,
    yrecv,
    rsend,
    rrecv,
    psend,
    precv,
    cpsend,
    cprecv,
    crsend,
    crrecv,
    cysend,
    cyrecv,
    cfsend,
    cfrecv,
):
    s, g, t, yh, z, yl, x = _here()
    y = yh * 2 + yl
    d = s * NT + t
    oh = 1 - yh

    def st_dev(e):
        return {"sect": e // NT, "tp": e % NT}

    def y_dev(e):
        return {"grp": (e // 2) * NZ + z, "tp": (e % 2) * NX + x}

    def z_dev(e):
        return {"grp": yh * NZ + e}

    def x_dev(e):
        return {"tp": yl * NX + e}

    def xy_dev(ex, ey):
        return {"grp": (ey // 2) * NZ + z, "tp": (ey % 2) * NX + ex}

    partner = {"sect": 1 - s}
    zr, zl = (z + 1) % NZ, (z + NZ - 1) % NZ
    xr, xl = (x + 1) % NX, (x + NX - 1) % NX
    xo = (x + 2) % NX

    chunk = BR // 2
    fetch = [
        pltpu.make_async_copy(
            cache_ref.at[pl.ds(chunk * q, chunk)], cbuf.at[pl.ds(chunk * q, chunk)], csem.at[q]
        )
        for q in range(2)
    ]
    fetch.append(pltpu.make_async_copy(vup_ref, vbuf, csem.at[2]))
    for c in (fetch[0], fetch[2], fetch[1]):
        c.start()
    loads = [
        pltpu.make_async_copy(wg_ref, wbuf.at[:, pl.ds(0, BC), pl.ds(0, 128)], wsem.at[0]),
        pltpu.make_async_copy(wu_ref, wbuf.at[:, pl.ds(0, BC), pl.ds(128, 128)], wsem.at[1]),
        pltpu.make_async_copy(wd_ref, wdraw, wsem.at[2]),
        pltpu.make_async_copy(
            wg_ref.at[:, pl.ds(384, 64)], wbuf.at[:, pl.ds(BC, 64), pl.ds(0, 128)], wsem.at[3]
        ),
        pltpu.make_async_copy(
            wu_ref.at[:, pl.ds(384, 64)], wbuf.at[:, pl.ds(BC, 64), pl.ds(128, 128)], wsem.at[4]
        ),
    ]
    for c in loads:
        c.start()

    expected = _signal_all(
        [st_dev((d + o) % NST) for o in range(1, NST)]
        + [z_dev((z + o) % NZ) for o in range(1, NZ)]
        + [y_dev((y + o) % NY) for o in range(1, NY)]
        + [{"grp": oh * NZ + z, "tp": (t + o) % NT} for o in range(1, NT)]
    )

    sent = []

    def start(c):
        c.start()
        sent.append(c)

    def landed(ref, sem):
        _remote(ref, ref, asend.at[0], sem, partner).wait_recv()


    steps = [z_dev((z + o) % NZ) for o in (1, NZ - 1, 2, NZ - 2)] + [{"grp": oh * NZ + z}]

    def hop(src, slot, q, way):
        start(_remote(src, gbuf.at[slot, q], hsend.at[slot, q, way], hrecv.at[slot, q], steps[way]))

    def attend(q):
        fetch[q].wait()
        heads = q_ref.shape[1]
        shape = (heads, cbuf.shape[2])
        positions = lax.broadcasted_iota(jnp.int32, shape, 1)
        for i in range(chunk):
            r = chunk * q + i
            score = jnp.dot(q_ref[r], cbuf[r], preferred_element_type=F32) * SOFTMAX_SCALE
            sbuf[i] = jnp.where(positions < len_ref[r], score, MASK_VALUE)
        score = sbuf[...]
        top = jnp.max(score, axis=2, keepdims=True)
        e = jnp.where(score > 0.5 * MASK_VALUE, jnp.exp(score - top), 0.0)
        sbuf[...] = e / jnp.sum(e, axis=2, keepdims=True)
        for i in range(chunk):
            r = chunk * q + i
            latent = lax.dot_general(
                sbuf[i].astype(BF16), cbuf[r, :LAT], (((1,), (1,)), ((), ())), preferred_element_type=F32
            )
            lbuf[i] = latent.astype(BF16).astype(F32)
        if q == 0:
            fetch[2].wait()
        for h in range(heads):
            value = jnp.dot(lbuf[:, h, :].astype(BF16), vbuf[h], preferred_element_type=F32)
            own_ref[q, :, VDIM * h : VDIM * (h + 1)] = value.astype(BF16)

    for q in range(2):
        attend(q)
        if q == 0:
            pl.semaphore_wait(pltpu.get_barrier_semaphore(), expected)
        for way in (4, 2, 3, 0, 1):
            hop(own_ref.at[q], g, q, way)

    for c in range(8):
        obuf[pl.ds(128 * c, 128), :] = oproj_ref[:, pl.ds(128 * c, 128)].T
    window = pl.multiple_of((d // 4) * 128, 128)
    resbuf[...] = res_ref[:, pl.ds(window, 128)].T
    pick = (ids_ref[...] == g).astype(F32) * wts_ref[...]
    wcol[...] = jnp.broadcast_to(jnp.sum(pick, axis=0, keepdims=True), (8, NST * BR)).T

    def project(slots, blocks):
        lhs = blocks[0] if len(blocks) == 1 else jnp.concatenate(blocks, axis=0)
        p = jnp.dot(lhs, obuf[...], preferred_element_type=F32).astype(BF16)
        for i, e in enumerate(slots):
            part[e] = p[i * BR : (i + 1) * BR]

            @pl.when(e != d)
            def _():
                _remote(part.at[e], rbuf.at[d], bsend.at[e], brecv.at[d], st_dev(e)).start()

    def block(slot):
        return gbuf[slot].reshape(BR, gbuf.shape[3])

    half = NZ // 2

    def arrive(side, k):
        slots = []
        for q in range(2):
            for way in range(1 if k in (0, half) else 2):
                slot = (yh, oh)[side] * NZ + (z + NZ - k if way == 0 else z + k) % NZ
                landed(gbuf.at[slot, q], hrecv.at[slot, q])
                if side == 0 and k == 2:
                    hop(gbuf.at[slot, q], slot, q, way)
                    if q == way:
                        hop(gbuf.at[slot, q], slot, q, 2 + way)
                if side == 0 and k > 2:
                    hop(gbuf.at[slot, q], slot, q, 4)
                if side == 1 and k == 0:
                    for w in (2, 3, 0, 1):
                        hop(gbuf.at[slot, q], slot, q, w)
                if q == 0:
                    slots.append(slot)
        return slots

    held, blocks = [g], [own_ref[...].reshape(BR, gbuf.shape[3])]
    for side, k, now in (
        (0, 1, 0),
        (0, 2, 0),
        (1, 0, 1),
        (0, 3, 0),
        (0, 4, 1),
        (1, 1, 0),
        (1, 2, 1),
        (1, 3, 1),
        (1, 4, 1),
    ):
        slots = arrive(side, k)
        held += slots
        blocks += [block(e) for e in slots]
        if now:
            project(held, blocks)
            held, blocks = [], []

    def twice(v, high):
        v = v.astype(F32)
        low = lax.broadcasted_iota(jnp.int32, v.shape, 1) < 64
        return jnp.where(low != high, v, pltpu.roll(v, 64, 1)).astype(BF16)

    for c in loads:
        c.wait()
    for i in range(8):
        v = wdraw[:, pl.ds(2 * BC * i, 2 * BC)]
        wdbuf[2 * i, :, :384] = v[:, :384]
        wdbuf[2 * i, :, 384:] = twice(v[:, 384:512], False)
        wdbuf[2 * i + 1, :, :384] = v[:, BC : BC + 384]
        wdbuf[2 * i + 1, :, 384:] = twice(v[:, 768:896], True)

    base = pl.multiple_of((d % 4) * BR, BR)
    total = resbuf[pl.ds(base, BR), :].astype(F32) + part[d].astype(F32)
    for o in range(1, NST):
        e = (d + NST - o) % NST
        landed(rbuf.at[e], brecv.at[e])
        total = total + rbuf[e].astype(F32)
    left_half = lax.broadcasted_iota(jnp.int32, (TILE, 128), 1) < 64
    tmp[...] = jnp.zeros_like(tmp)
    tmp[:, :BC] = total
    tails = tmp[:, 384:]
    own_tiles = [tmp[TILE * r : TILE * (r + 1), 128 * c : 128 * (c + 1)] for r in range(2) for c in range(3)]
    own_tiles.append(jnp.where(left_half, tails[:TILE], pltpu.roll(tails[TILE:], 64, 1)))
    packed = jnp.concatenate(own_tiles, axis=0).astype(BF16)
    mine[...] = packed
    rows[yh, z, s, t] = packed
    hacc[...] = jnp.zeros_like(hacc)

    def weights(hh, zz):
        return wbuf[hh * NZ + zz]

    def matrix(blocks):
        lanes = lax.broadcasted_iota(jnp.int32, (TILE, 128), 1) < 64

        def tile(b, i):
            return b[TILE * i : TILE * (i + 1), :]

        columns = [
            jnp.concatenate([tile(b, 3 * r + c) for b in blocks for r in range(2)], axis=0) for c in range(3)
        ]
        last = []
        for b in blocks:
            v = tile(b, 6)
            last += [jnp.where(lanes, v, jnp.zeros_like(v)), jnp.where(lanes, jnp.zeros_like(v), v)]
        return jnp.concatenate(columns + [jnp.concatenate(last, axis=0)], axis=1)

    def put(dst, p):
        for r in range(2):
            for c in range(3):
                n = 3 * r + c
                dst[TILE * n : TILE * (n + 1), :] = p[TILE * r : TILE * (r + 1), 128 * c : 128 * (c + 1)].astype(
                    BF16
                )
        dst[TILE * 6 :, :] = jnp.where(left_half, p[:TILE, 384:], p[TILE:, 384:]).astype(BF16)

    def use_plane(k):
        count = 2 if k in (0, half) else 4

        def step(i, carry):
            hh = i % 2
            zz = (z + (i // 2) * 2 * k + NZ - k) % NZ
            a = matrix([rows.at[hh, zz, 1, e] for e in range(NT)])
            p = jnp.dot(a, weights(hh, zz), preferred_element_type=F32)
            hacc[1] += p.reshape(8, BR, 256)
            return carry

        lax.fori_loop(0, count, step, 0)

    def use_group(*xx):
        places = [o + e for e in xx for o in (0, NX)]

        def step(i, carry):
            hh = i // NZ
            zz = i % NZ
            a = matrix([rows.at[hh, zz, 0, e] for e in places])
            return carry + jnp.dot(a, weights(hh, zz), preferred_element_type=F32)

        p = lax.fori_loop(0, NG, step, jnp.zeros((len(places) * BR, 256), F32))
        for i, e in enumerate(places):
            hacc[0, e] = p[i * BR : (i + 1) * BR]

    ymine = (y, (y + NY - 1) % NY, (y + 1) % NY, (y + 2) % NY)

    def quad_of(zz, yy):
        return rows.at[yy // 2, zz, 1, pl.ds((yy % 2) * NX, NX)]

    def qid(k, way, j):
        return j if k == 0 else 8 * k - 4 + 4 * way + j

    @pl.when(s == 0)
    def _():
        def piece(xx, yy):
            return rows.at[yy // 2, :, 0, (yy % 2) * NX + xx]

        mark = len(sent)
        b = rows.at[yh, z, 0, t]
        for o in range(1, NZ):
            start(_remote(b, b, ssend.at[o], srecv.at[z], z_dev((z + o) % NZ)))
        for o in range(1, NZ):
            e = (z + NZ - o) % NZ
            landed(rows.at[yh, e, 0, t], srecv.at[e])

        def to_partner(p, i):
            start(_remote(p, p, psend.at[i], precv.at[i], partner))

        def other(k):
            for j in range(4):
                for way in range(1 if k in (0, half) else 2):
                    landed(quad_of((z + NZ - k if way == 0 else z + k) % NZ, ymine[j]), precv.at[qid(k, way, j)])
            use_plane(k)

        yr, yl_ = y_dev((y + 1) % NY), y_dev((y + NY - 1) % NY)
        p = piece(x, y)
        start(_remote(p, p, ysend.at[0], yrecv.at[0], yr))
        start(_remote(p, p, ysend.at[1], yrecv.at[1], yl_))

        def out(j):
            q = piece(x, ymine[j])
            start(_remote(q, q, rsend.at[0, j], rrecv.at[0, j], x_dev(xr)))
            start(_remote(q, q, rsend.at[1, j], rrecv.at[1, j], x_dev(xl)))
            to_partner(q, j)

        def halfof(w):
            yy = ymine[(1, 2)[w]]
            return rows.at[yy // 2, pl.ds(4 * w, 4), 0, (yy % 2) * NX + x]

        def halfin(w):
            yy = ymine[3]
            return rows.at[yy // 2, pl.ds(4 * w, 4), 0, (yy % 2) * NX + x]

        def ring_in(j):
            q = piece(xl, ymine[j])
            landed(q, rrecv.at[0, j])
            if j % 2 == 0:
                start(_remote(q, q, rsend.at[0, 4 + j], rrecv.at[0, 4 + j], x_dev(xr)))
            to_partner(q, 4 + j)
            q = piece(xr, ymine[j])
            landed(q, rrecv.at[1, j])
            if j % 2 == 1:
                start(_remote(q, q, rsend.at[1, 4 + j], rrecv.at[1, 4 + j], x_dev(xl)))
            to_partner(q, 8 + j)

        out(0)
        for w in range(2):
            landed(piece(x, ymine[1 + w]), yrecv.at[w])
            q = halfof(w)
            start(_remote(q, q, ysend.at[2 + w], yrecv.at[2 + w], (yr, yl_)[w]))
            out(1 + w)
        ring_in(0)
        for w in range(2):
            landed(halfin(w), yrecv.at[2 + w])
        out(3)
        use_group(x)
        ring_in(1)
        ring_in(2)
        other(0)
        ring_in(3)
        use_group(xl, xr)
        other(1)
        for j in range(4):
            p = piece(xo, ymine[j])
            landed(p, rrecv.at[j % 2, 4 + j])
            to_partner(p, 12 + j)
        use_group(xo)
        for k in range(2, half + 1):
            other(k)
        for c in sent[mark:]:
            c.wait_send()
        del sent[mark:]

    @pl.when(s == 1)
    def _():
        def piece(zz, hh):
            return rows.at[hh, zz, 1]

        mark = len(sent)
        b = rows.at[yh, z, 1, t]
        for oy in (0, 1, 3, 2):
            for ox in range(NX):
                if oy + ox:
                    n = oy * NX + ox
                    start(_remote(b, b, ssend.at[n], srecv.at[n], xy_dev((x + ox) % NX, (y + oy) % NY)))

        def to_partner(p, i):
            start(_remote(p, p, psend.at[i], precv.at[i], partner))

        def other(i, *xx):
            for e in xx:
                for j in range(4):
                    yy = ymine[j]
                    landed(rows.at[yy // 2, :, 0, (yy % 2) * NX + e], precv.at[4 * i + j])
                i = i + 1
            use_group(*xx)

        def out(j):
            q = quad_of(z, ymine[j])
            start(_remote(q, q, rsend.at[0, j], rrecv.at[0, j], z_dev(zr)))
            start(_remote(q, q, rsend.at[1, j], rrecv.at[1, j], z_dev(zl)))
            to_partner(q, qid(0, 0, j))

        def ring_in(k, j):
            n = 4 * k + j
            for way in range(2):
                if k == half and j % 2 != way:
                    continue
                q = quad_of((z + NZ - k if way == 0 else z + k) % NZ, ymine[j])
                landed(q, rrecv.at[way, n - 4])
                if k < half - 1 or (k == half - 1 and j % 2 == way):
                    start(_remote(q, q, rsend.at[way, n], rrecv.at[way, n], z_dev((zr, zl)[way])))
                to_partner(q, qid(k, 0 if k == half else way, j))

        for j, oy in enumerate((0, 1, 3, 2)):
            yy = ymine[j]
            for ox in range(NX):
                if oy + ox:
                    n = oy * NX + ox
                    landed(rows.at[yy // 2, z, 1, (yy % 2) * NX + (x + NX - ox) % NX], srecv.at[n])
            out(j)
        use_plane(0)
        for k in range(1, half + 1):
            for j in range(4):
                ring_in(k, j)
            if k < half:
                use_plane(k)
            if k == 2:
                other(0, x)
            if k == 3:
                other(1, xl, xr)
        use_plane(half)
        other(3, xo)
        for c in sent[mark:]:
            c.wait_send()
        del sent[mark:]

    gate = hacc[:, :, :, :128].reshape(NST * BR, 128)
    up = hacc[:, :, :, 128:].reshape(NST * BR, 128)
    weight = wcol[:, 0:1]
    hid[...] = (weight * (gate / (1.0 + jnp.exp(-gate))) * up).astype(BF16).reshape(2, NT, BR, 128)

    def down_plane(dst, sec, zz, hh):
        a = hid[sec].reshape(NT * BR, 128)
        p = jnp.dot(a, wdbuf[hh * NZ + zz], preferred_element_type=F32)
        for e in range(NT):
            put(dst.at[hh, zz, e], p[BR * e : BR * (e + 1)])

    def down_group(dst, sec, xx):
        a = jnp.concatenate([hid[sec, xx], hid[sec, NX + xx]], axis=0)

        def step(i, carry):
            p = jnp.dot(a, wdbuf[i], preferred_element_type=F32)
            put(dst.at[i // NZ, i % NZ, xx], p[:BR])
            put(dst.at[i // NZ, i % NZ, NX + xx], p[BR:])
            return carry

        lax.fori_loop(0, NG, step, 0)

    def add(dst, srcs, n=8):
        def step(i, carry):
            v = dst[i].astype(F32)
            for r in srcs:
                v = v + r[i].astype(F32)
            dst[i] = v.astype(BF16)
            return carry

        lax.fori_loop(0, n, step, 0)

    def finish(refs):
        tot = refs[0][...].astype(F32)
        for r in refs[1:]:
            tot = tot + r[...].astype(F32)
        tot = mine[...].astype(F32) + tot
        for r in range(2):
            for c in range(3):
                n = TILE * (3 * r + c)
                out_ref[TILE * r : TILE * (r + 1), 128 * c : 128 * (c + 1)] = tot[n : n + TILE].astype(BF16)
        tails = tot[6 * TILE :]
        out_ref[:TILE, 384:] = tails[:, :64].astype(BF16)
        out_ref[TILE:, 384:] = pltpu.roll(tails, 64, 1)[:, :64].astype(BF16)

    xs = (xo, xr, xl, x)
    zs = [(z + half) % NZ]
    for k in range(half - 1, 0, -1):
        zs += [(z + k) % NZ, (z + NZ - k) % NZ]
    zs.append(z)
    ys = ((y + 2) % NY, (y + 1) % NY, (y + NY - 1) % NY, y)
    yright, yleft = y_dev((y + 1) % NY), y_dev((y + NY - 1) % NY)

    def quad(ref, i, j):
        return ref.at[ys[j] // 2, zs[i], pl.ds((ys[j] % 2) * NX, NX)]

    @pl.when(s == 0)
    def _():
        mark = len(sent)

        def give(i):
            for h in range(2):
                down_plane(tsend, 1, zs[i], h)
            for j in range(4):
                n = 4 * i + j
                start(_remote(quad(tsend, i, j), quad(pbuf, i, j), cpsend.at[n], cprecv.at[n], partner))

        def at(ref, i, j):
            yy = ys[j]
            return ref.at[yy // 2, :, (yy % 2) * NX + xs[i]]

        def take(i, j, more=()):
            landed(at(pbuf, i, j), cprecv.at[4 * i + j])
            add(at(acc, i, j), [at(pbuf, i, j)] + list(more))

        right, left = x_dev(xr), x_dev(xl)
        give(0)
        down_group(acc, 0, xs[0])
        give(1)
        for j in range(4):
            take(0, j)
            start(_remote(at(acc, 0, j), ring.at[j], crsend.at[j], crrecv.at[j], right if j % 2 == 0 else left))
        down_group(acc, 0, xs[1])
        give(2)
        down_group(acc, 0, xs[2])
        give(3)
        for j in range(4):
            for i, way, dev in ((1, 0, right), (2, 1, left)):
                if j % 2 == way:
                    landed(ring.at[j], crrecv.at[j])
                    take(i, j, [ring.at[j]])
                else:
                    take(i, j)
                k = 4 + 4 * way + j
                start(_remote(at(acc, i, j), ring.at[k], crsend.at[k], crrecv.at[k], dev))
            give(4 + j)
        down_group(acc, 0, xs[3])
        for j in range(4):
            landed(ring.at[4 + j], crrecv.at[4 + j])
            landed(ring.at[8 + j], crrecv.at[8 + j])
            take(3, j, [ring.at[4 + j], ring.at[8 + j]])
            yy = ys[j]
            tt = (yy % 2) * NX + x
            if j == 0:
                for w in range(2):
                    part4 = pl.ds(4 * w, 4)
                    start(
                        _remote(
                            acc.at[yy // 2, part4, tt],
                            ybuf.at[0, part4],
                            cysend.at[w],
                            cyrecv.at[w],
                            (yright, yleft)[w],
                        )
                    )
            elif j < 3:
                w = j - 1
                part4 = pl.ds(4 * w, 4)
                landed(ybuf.at[0, part4], cyrecv.at[w])
                add(acc.at[yy // 2, part4, tt], [ybuf.at[0, part4]], 4)
                start(
                    _remote(at(acc, 3, j), ybuf.at[j], cysend.at[1 + j], cyrecv.at[1 + j], (yright, yleft)[w])
                )
        for j in (1, 2):
            landed(ybuf.at[j], cyrecv.at[1 + j])
        add(at(acc, 3, 3), [ybuf.at[1], ybuf.at[2]])
        for o in range(1, NZ):
            e = (z + o) % NZ
            start(_remote(acc.at[yh, e, t], fbuf.at[o], cfsend.at[o], cfrecv.at[o], z_dev(e)))
        for o in range(1, NZ):
            landed(fbuf.at[o], cfrecv.at[o])
        finish([acc.at[yh, z, t]] + [fbuf.at[o] for o in range(1, NZ)])
        for c in sent[mark:]:
            c.wait_send()
        del sent[mark:]

    @pl.when(s == 1)
    def _():
        mark = len(sent)

        def give(i):
            down_group(tsend, 0, xs[i])
            for j, yy in enumerate(ys):
                tt = (yy % 2) * NX + xs[i]
                n = 4 * i + j
                start(
                    _remote(tsend.at[yy // 2, :, tt], pbuf.at[yy // 2, :, tt], cpsend.at[n], cprecv.at[n], partner)
                )

        def have(i):
            for h in range(2):
                down_plane(acc, 1, zs[i], h)

        def take(i, j, more=()):
            landed(quad(pbuf, i, j), cprecv.at[4 * i + j])
            add(quad(acc, i, j), [quad(pbuf, i, j)] + list(more), NX)

        def slot(n):
            return ring.at[n // 2, pl.ds((n % 2) * NX, NX)]

        right, left = z_dev(zr), z_dev(zl)
        give(0)
        have(0)
        for j in range(4):
            take(0, j)
            start(_remote(quad(acc, 0, j), slot(j), crsend.at[j], crrecv.at[j], (right, left)[j % 2]))
        have(1)
        have(2)
        give(1)
        for k in range(1, half):
            for j in range(4):
                for way, dev in ((0, right), (1, left)):
                    i = 2 * k - 1 + way
                    prev = 4 + 8 * (k - 2) + 4 * way + j
                    if k == 1:
                        prev = j if j % 2 == way else None
                    if prev is None:
                        take(i, j)
                    else:
                        landed(slot(prev), crrecv.at[prev])
                        take(i, j, [slot(prev)])
                    q = 4 + 8 * (k - 1) + 4 * way + j
                    start(_remote(quad(acc, i, j), slot(q), crsend.at[q], crrecv.at[q], dev))
            if k == 1:
                give(2)
                give(3)
            have(2 * k + 1)
            if k < half - 1:
                have(2 * k + 2)

        for j in range(4):
            q = 4 + 8 * (half - 2) + j
            landed(slot(q), crrecv.at[q])
            landed(slot(q + 4), crrecv.at[q + 4])
            take(7, j, [slot(q), slot(q + 4)])
            oy = (2, 1, 3, 0)[j]
            for ox in range(NX):
                if oy + ox:
                    n = oy * NX + ox
                    ex = (x + ox) % NX
                    src = acc.at[ys[j] // 2, z, (ys[j] % 2) * NX + ex]
                    start(_remote(src, fbuf.at[n], cfsend.at[n], cfrecv.at[n], xy_dev(ex, ys[j])))
        for n in range(1, NY * NX):
            landed(fbuf.at[n], cfrecv.at[n])
        finish([acc.at[yh, z, t]] + [fbuf.at[n] for n in range(1, NY * NX)])
        for c in sent[mark:]:
            c.wait_send()
        del sent[mark:]

    for o in range(1, NST):
        e = (d + o) % NST
        _remote(part.at[e], rbuf.at[d], bsend.at[e], brecv.at[d], st_dev(e)).wait_send()
    for c in sent:
        c.wait_send()


def layer(queries, latent_cache, cache_len, value_up, out_proj, residual, w_gate, w_up, w_down, route_ids, route_weights):
    vmem = pl.BlockSpec(memory_space=pltpu.VMEM)
    hbm = pl.BlockSpec(memory_space=pl.ANY)
    dma = pltpu.SemaphoreType.DMA
    depth = value_up.shape[0] * VDIM
    scratch = [
        pltpu.VMEM((BR, latent_cache.shape[2], latent_cache.shape[1]), BF16),
        pltpu.VMEM(value_up.shape, BF16),
        pltpu.VMEM((BR // 2, queries.shape[1], latent_cache.shape[1]), F32),
        pltpu.VMEM((BR // 2, queries.shape[1], LAT), F32),
        pltpu.VMEM((2, BR // 2, depth), BF16),
        pltpu.VMEM((NG, 2, BR // 2, depth), BF16),
        pltpu.VMEM((depth, BC), BF16),
        pltpu.VMEM((NG, WIDE, 256), BF16),
        pltpu.VMEM(w_down.shape, BF16),
        pltpu.VMEM((NG, 128, WIDE), BF16),
        pltpu.VMEM((128, BC), BF16),
        pltpu.VMEM((NST * BR, 8), F32),
        pltpu.VMEM((NST, BR, BC), BF16),
        pltpu.VMEM((NST, BR, BC), BF16),
        pltpu.VMEM((PACK, 128), BF16),
        pltpu.VMEM((2, NZ, 2, NT, PACK, 128), BF16),
        pltpu.VMEM((2, NT, BR, 256), F32),
        pltpu.VMEM((2, NT, BR, 128), BF16),
        pltpu.VMEM((2, NZ, NT, PACK, 128), BF16),
        pltpu.VMEM((2, NZ, NT, PACK, 128), BF16),
        pltpu.VMEM((2, NZ, NT, PACK, 128), BF16),
        pltpu.VMEM((16, 8, PACK, 128), BF16),
        pltpu.VMEM((3, 8, PACK, 128), BF16),
        pltpu.VMEM((16, PACK, 128), BF16),
        pltpu.VMEM((BR, WIDE), F32),
        dma((3,)),
        dma((5,)),
        dma((NG, 2, 5)),
        dma((NG, 2)),
        dma((1,)),
        dma((NST,)),
        dma((NST,)),
        dma((16,)),
        dma((16,)),
        dma((NY,)),
        dma((NY,)),
        dma((2, 16)),
        dma((2, 16)),
        dma((32,)),
        dma((32,)),
        dma((32,)),
        dma((32,)),
        dma((28,)),
        dma((28,)),
        dma((4,)),
        dma((4,)),
        dma((16,)),
        dma((16,)),
    ]
    return pl.pallas_call(
        _layer_kernel,
        out_shape=jax.ShapeDtypeStruct((BR, BC), BF16),
        in_specs=[pl.BlockSpec(memory_space=pltpu.SMEM), vmem, hbm, hbm, vmem, vmem, hbm, hbm, hbm, vmem, vmem],
        out_specs=vmem,
        scratch_shapes=scratch,
        compiler_params=pltpu.CompilerParams(
            collective_id=0, has_side_effects=True, vmem_limit_bytes=60 * 1024 * 1024
        ),
        name="layer",
    )(
        cache_len,
        queries,
        latent_cache.transpose(0, 2, 1),
        value_up,
        out_proj.T,
        residual.T,
        w_gate.reshape(NG, BC, 128),
        w_up.reshape(NG, BC, 128),
        w_down,
        route_ids.T,
        route_weights.T,
    )


def on_device(
    queries,
    latent_cache,
    cache_len,
    value_up,
    out_proj,
    residual,
    w_gate,
    w_up,
    w_down,
    route_ids,
    route_weights,
):
    return layer(
        queries,
        latent_cache,
        cache_len,
        value_up,
        out_proj,
        residual,
        w_gate[0],
        w_up[0],
        w_down[0],
        route_ids,
        route_weights,
    )


def solution(mesh):
    return jax.shard_map(
        on_device,
        mesh=mesh,
        in_specs=(
            P("grp", ("sect", "tp"), None),
            P("grp", None, None),
            P("grp"),
            P(("sect", "tp"), None, None),
            P(("sect", "tp"), "grp"),
            P(None, "grp"),
            P("grp", None, ("sect", "tp")),
            P("grp", None, ("sect", "tp")),
            P("grp", ("sect", "tp"), None),
            P(),
            P(),
        ),
        out_specs=P(("sect", "tp"), "grp"),
        check_vma=False,
    )
```

```python
import jax
import jax.numpy as jnp
from jax import lax
from jax.experimental import pallas as pl
from jax.experimental.pallas import tpu as pltpu
from jax.sharding import PartitionSpec as P

LAT = 512
VDIM = 128
NX = 4
NY = 4
NZ = 8
NT = 8
NG = 16
NST = 16
BR = 32
BC = 448
TILE = 16
PACK = 7 * TILE
WIDE = 512

SOFTMAX_SCALE = 0.0721688
MASK_VALUE = -1e30
MESH = pl.DeviceIdType.MESH
BF16 = jnp.bfloat16
F32 = jnp.float32


def _here():
    s = lax.axis_index("sect")
    g = lax.axis_index("grp")
    t = lax.axis_index("tp")
    yh, z = g // NZ, g % NZ
    yl, x = t // NX, t % NX
    return s, g, t, yh, z, yl, x


def _remote(src, dst, send, recv, dev):
    return pltpu.make_async_remote_copy(
        src_ref=src, dst_ref=dst, send_sem=send, recv_sem=recv, device_id=dev, device_id_type=MESH
    )


def _signal_all(devs):
    for dev in devs:
        pl.semaphore_signal(pltpu.get_barrier_semaphore(), inc=1, device_id=dev, device_id_type=MESH)
    return len(devs)


def _layer_kernel(
    len_ref,
    q_ref,
    cache_ref,
    vup_ref,
    oproj_ref,
    res_ref,
    wg_ref,
    wu_ref,
    wd_ref,
    ids_ref,
    wts_ref,
    out_ref,
    cbuf,
    vbuf,
    sbuf,
    lbuf,
    own_ref,
    gbuf,
    obuf,
    wbuf,
    wdraw,
    wdbuf,
    resbuf,
    wcol,
    part,
    rbuf,
    mine,
    rows,
    hacc,
    hid,
    tsend,
    pbuf,
    acc,
    ring,
    ybuf,
    fbuf,
    tmp,
    csem,
    wsem,
    hsend,
    hrecv,
    asend,
    bsend,
    brecv,
    ssend,
    srecv,
    ysend,
    yrecv,
    rsend,
    rrecv,
    psend,
    precv,
    cpsend,
    cprecv,
    crsend,
    crrecv,
    cysend,
    cyrecv,
    cfsend,
    cfrecv,
):
    s, g, t, yh, z, yl, x = _here()
    y = yh * 2 + yl
    d = s * NT + t
    oh = 1 - yh

    def st_dev(e):
        return {"sect": e // NT, "tp": e % NT}

    def y_dev(e):
        return {"grp": (e // 2) * NZ + z, "tp": (e % 2) * NX + x}

    def z_dev(e):
        return {"grp": yh * NZ + e}

    def x_dev(e):
        return {"tp": yl * NX + e}

    def xy_dev(ex, ey):
        return {"grp": (ey // 2) * NZ + z, "tp": (ey % 2) * NX + ex}

    partner = {"sect": 1 - s}
    zr, zl = (z + 1) % NZ, (z + NZ - 1) % NZ
    xr, xl = (x + 1) % NX, (x + NX - 1) % NX
    xo = (x + 2) % NX

    chunk = BR // 2
    fetch = [
        pltpu.make_async_copy(
            cache_ref.at[pl.ds(chunk * q, chunk)], cbuf.at[pl.ds(chunk * q, chunk)], csem.at[q]
        )
        for q in range(2)
    ]
    fetch.append(pltpu.make_async_copy(vup_ref, vbuf, csem.at[2]))
    for c in (fetch[0], fetch[2], fetch[1]):
        c.start()
    loads = [
        pltpu.make_async_copy(wg_ref, wbuf.at[:, pl.ds(0, BC), pl.ds(0, 128)], wsem.at[0]),
        pltpu.make_async_copy(wu_ref, wbuf.at[:, pl.ds(0, BC), pl.ds(128, 128)], wsem.at[1]),
        pltpu.make_async_copy(wd_ref, wdraw, wsem.at[2]),
        pltpu.make_async_copy(
            wg_ref.at[:, pl.ds(384, 64)], wbuf.at[:, pl.ds(BC, 64), pl.ds(0, 128)], wsem.at[3]
        ),
        pltpu.make_async_copy(
            wu_ref.at[:, pl.ds(384, 64)], wbuf.at[:, pl.ds(BC, 64), pl.ds(128, 128)], wsem.at[4]
        ),
    ]
    for c in loads:
        c.start()

    expected = _signal_all(
        [st_dev((d + o) % NST) for o in range(1, NST)]
        + [z_dev((z + o) % NZ) for o in range(1, NZ)]
        + [y_dev((y + o) % NY) for o in range(1, NY)]
        + [{"grp": oh * NZ + z, "tp": (t + o) % NT} for o in range(1, NT)]
    )

    sent = []

    def start(c):
        c.start()
        sent.append(c)

    def landed(ref, sem):
        _remote(ref, ref, asend.at[0], sem, partner).wait_recv()


    steps = [z_dev((z + o) % NZ) for o in (1, NZ - 1, 2, NZ - 2)] + [{"grp": oh * NZ + z}]

    def hop(src, slot, q, way):
        start(_remote(src, gbuf.at[slot, q], hsend.at[slot, q, way], hrecv.at[slot, q], steps[way]))

    def attend(q):
        fetch[q].wait()
        heads = q_ref.shape[1]
        shape = (heads, cbuf.shape[2])
        positions = lax.broadcasted_iota(jnp.int32, shape, 1)
        for i in range(chunk):
            r = chunk * q + i
            score = jnp.dot(q_ref[r], cbuf[r], preferred_element_type=F32) * SOFTMAX_SCALE
            sbuf[i] = jnp.where(positions < len_ref[r], score, MASK_VALUE)
        score = sbuf[...]
        top = jnp.max(score, axis=2, keepdims=True)
        e = jnp.where(score > 0.5 * MASK_VALUE, jnp.exp(score - top), 0.0)
        sbuf[...] = e / jnp.sum(e, axis=2, keepdims=True)
        for i in range(chunk):
            r = chunk * q + i
            latent = lax.dot_general(
                sbuf[i].astype(BF16), cbuf[r, :LAT], (((1,), (1,)), ((), ())), preferred_element_type=F32
            )
            lbuf[i] = latent.astype(BF16).astype(F32)
        if q == 0:
            fetch[2].wait()
        for h in range(heads):
            value = jnp.dot(lbuf[:, h, :].astype(BF16), vbuf[h], preferred_element_type=F32)
            own_ref[q, :, VDIM * h : VDIM * (h + 1)] = value.astype(BF16)

    for q in range(2):
        attend(q)
        if q == 0:
            pl.semaphore_wait(pltpu.get_barrier_semaphore(), expected)
        for way in (4, 2, 3, 0, 1):
            hop(own_ref.at[q], g, q, way)

    for c in range(8):
        obuf[pl.ds(128 * c, 128), :] = oproj_ref[:, pl.ds(128 * c, 128)].T
    window = pl.multiple_of((d // 4) * 128, 128)
    resbuf[...] = res_ref[:, pl.ds(window, 128)].T
    pick = (ids_ref[...] == g).astype(F32) * wts_ref[...]
    wcol[...] = jnp.broadcast_to(jnp.sum(pick, axis=0, keepdims=True), (8, NST * BR)).T

    def project(slots, blocks):
        lhs = blocks[0] if len(blocks) == 1 else jnp.concatenate(blocks, axis=0)
        p = jnp.dot(lhs, obuf[...], preferred_element_type=F32).astype(BF16)
        for i, e in enumerate(slots):
            part[e] = p[i * BR : (i + 1) * BR]

            @pl.when(e != d)
            def _():
                _remote(part.at[e], rbuf.at[d], bsend.at[e], brecv.at[d], st_dev(e)).start()

    def block(slot):
        return gbuf[slot].reshape(BR, gbuf.shape[3])

    half = NZ // 2

    def arrive(side, k):
        slots = []
        for q in range(2):
            for way in range(1 if k in (0, half) else 2):
                slot = (yh, oh)[side] * NZ + (z + NZ - k if way == 0 else z + k) % NZ
                landed(gbuf.at[slot, q], hrecv.at[slot, q])
                if side == 0 and k == 2:
                    hop(gbuf.at[slot, q], slot, q, way)
                    if q == way:
                        hop(gbuf.at[slot, q], slot, q, 2 + way)
                if side == 0 and k > 2:
                    hop(gbuf.at[slot, q], slot, q, 4)
                if side == 1 and k == 0:
                    for w in (2, 3, 0, 1):
                        hop(gbuf.at[slot, q], slot, q, w)
                if q == 0:
                    slots.append(slot)
        return slots

    held, blocks = [g], [own_ref[...].reshape(BR, gbuf.shape[3])]
    for side, k, now in (
        (0, 1, 0),
        (0, 2, 0),
        (1, 0, 1),
        (0, 3, 0),
        (0, 4, 1),
        (1, 1, 0),
        (1, 2, 1),
        (1, 3, 1),
        (1, 4, 1),
    ):
        slots = arrive(side, k)
        held += slots
        blocks += [block(e) for e in slots]
        if now:
            project(held, blocks)
            held, blocks = [], []

    def twice(v, high):
        v = v.astype(F32)
        low = lax.broadcasted_iota(jnp.int32, v.shape, 1) < 64
        return jnp.where(low != high, v, pltpu.roll(v, 64, 1)).astype(BF16)

    for c in loads:
        c.wait()
    for i in range(8):
        v = wdraw[:, pl.ds(2 * BC * i, 2 * BC)]
        wdbuf[2 * i, :, :384] = v[:, :384]
        wdbuf[2 * i, :, 384:] = twice(v[:, 384:512], False)
        wdbuf[2 * i + 1, :, :384] = v[:, BC : BC + 384]
        wdbuf[2 * i + 1, :, 384:] = twice(v[:, 768:896], True)

    base = pl.multiple_of((d % 4) * BR, BR)
    total = resbuf[pl.ds(base, BR), :].astype(F32) + part[d].astype(F32)
    for o in range(1, NST):
        e = (d + NST - o) % NST
        landed(rbuf.at[e], brecv.at[e])
        total = total + rbuf[e].astype(F32)
    left_half = lax.broadcasted_iota(jnp.int32, (TILE, 128), 1) < 64
    tmp[...] = jnp.zeros_like(tmp)
    tmp[:, :BC] = total
    tails = tmp[:, 384:]
    own_tiles = [tmp[TILE * r : TILE * (r + 1), 128 * c : 128 * (c + 1)] for r in range(2) for c in range(3)]
    own_tiles.append(jnp.where(left_half, tails[:TILE], pltpu.roll(tails[TILE:], 64, 1)))
    packed = jnp.concatenate(own_tiles, axis=0).astype(BF16)
    mine[...] = packed
    rows[yh, z, s, t] = packed
    hacc[...] = jnp.zeros_like(hacc)

    def weights(hh, zz):
        return wbuf[hh * NZ + zz]

    def matrix(blocks):
        lanes = lax.broadcasted_iota(jnp.int32, (TILE, 128), 1) < 64

        def tile(b, i):
            return b[TILE * i : TILE * (i + 1), :]

        columns = [
            jnp.concatenate([tile(b, 3 * r + c) for b in blocks for r in range(2)], axis=0) for c in range(3)
        ]
        last = []
        for b in blocks:
            v = tile(b, 6)
            last += [jnp.where(lanes, v, jnp.zeros_like(v)), jnp.where(lanes, jnp.zeros_like(v), v)]
        return jnp.concatenate(columns + [jnp.concatenate(last, axis=0)], axis=1)

    def put(dst, p):
        for r in range(2):
            for c in range(3):
                n = 3 * r + c
                dst[TILE * n : TILE * (n + 1), :] = p[TILE * r : TILE * (r + 1), 128 * c : 128 * (c + 1)].astype(
                    BF16
                )
        dst[TILE * 6 :, :] = jnp.where(left_half, p[:TILE, 384:], p[TILE:, 384:]).astype(BF16)

    def use_plane(k):
        count = 2 if k in (0, half) else 4

        def step(i, carry):
            hh = i % 2
            zz = (z + (i // 2) * 2 * k + NZ - k) % NZ
            a = matrix([rows.at[hh, zz, 1, e] for e in range(NT)])
            p = jnp.dot(a, weights(hh, zz), preferred_element_type=F32)
            hacc[1] += p.reshape(8, BR, 256)
            return carry

        lax.fori_loop(0, count, step, 0)

    def use_group(*xx):
        places = [o + e for e in xx for o in (0, NX)]

        def step(i, carry):
            hh = i // NZ
            zz = i % NZ
            a = matrix([rows.at[hh, zz, 0, e] for e in places])
            return carry + jnp.dot(a, weights(hh, zz), preferred_element_type=F32)

        p = lax.fori_loop(0, NG, step, jnp.zeros((len(places) * BR, 256), F32))
        for i, e in enumerate(places):
            hacc[0, e] = p[i * BR : (i + 1) * BR]

    ymine = (y, (y + NY - 1) % NY, (y + 1) % NY, (y + 2) % NY)

    def quad_of(zz, yy):
        return rows.at[yy // 2, zz, 1, pl.ds((yy % 2) * NX, NX)]

    def qid(k, way, j):
        return j if k == 0 else 8 * k - 4 + 4 * way + j

    @pl.when(s == 0)
    def _():
        def piece(xx, yy):
            return rows.at[yy // 2, :, 0, (yy % 2) * NX + xx]

        mark = len(sent)
        b = rows.at[yh, z, 0, t]
        for o in range(1, NZ):
            start(_remote(b, b, ssend.at[o], srecv.at[z], z_dev((z + o) % NZ)))
        for o in range(1, NZ):
            e = (z + NZ - o) % NZ
            landed(rows.at[yh, e, 0, t], srecv.at[e])

        def to_partner(p, i):
            start(_remote(p, p, psend.at[i], precv.at[i], partner))

        def other(k):
            for j in range(4):
                for way in range(1 if k in (0, half) else 2):
                    landed(quad_of((z + NZ - k if way == 0 else z + k) % NZ, ymine[j]), precv.at[qid(k, way, j)])
            use_plane(k)

        yr, yl_ = y_dev((y + 1) % NY), y_dev((y + NY - 1) % NY)
        p = piece(x, y)
        start(_remote(p, p, ysend.at[0], yrecv.at[0], yr))
        start(_remote(p, p, ysend.at[1], yrecv.at[1], yl_))

        def out(j):
            q = piece(x, ymine[j])
            start(_remote(q, q, rsend.at[0, j], rrecv.at[0, j], x_dev(xr)))
            start(_remote(q, q, rsend.at[1, j], rrecv.at[1, j], x_dev(xl)))
            to_partner(q, j)

        def halfof(w):
            yy = ymine[(1, 2)[w]]
            return rows.at[yy // 2, pl.ds(4 * w, 4), 0, (yy % 2) * NX + x]

        def halfin(w):
            yy = ymine[3]
            return rows.at[yy // 2, pl.ds(4 * w, 4), 0, (yy % 2) * NX + x]

        def ring_in(j):
            q = piece(xl, ymine[j])
            landed(q, rrecv.at[0, j])
            if j % 2 == 0:
                start(_remote(q, q, rsend.at[0, 4 + j], rrecv.at[0, 4 + j], x_dev(xr)))
            to_partner(q, 4 + j)
            q = piece(xr, ymine[j])
            landed(q, rrecv.at[1, j])
            if j % 2 == 1:
                start(_remote(q, q, rsend.at[1, 4 + j], rrecv.at[1, 4 + j], x_dev(xl)))
            to_partner(q, 8 + j)

        out(0)
        for w in range(2):
            landed(piece(x, ymine[1 + w]), yrecv.at[w])
            q = halfof(w)
            start(_remote(q, q, ysend.at[2 + w], yrecv.at[2 + w], (yr, yl_)[w]))
            out(1 + w)
        ring_in(0)
        for w in range(2):
            landed(halfin(w), yrecv.at[2 + w])
        out(3)
        use_group(x)
        ring_in(1)
        ring_in(2)
        other(0)
        ring_in(3)
        use_group(xl, xr)
        other(1)
        for j in range(4):
            p = piece(xo, ymine[j])
            landed(p, rrecv.at[j % 2, 4 + j])
            to_partner(p, 12 + j)
        use_group(xo)
        for k in range(2, half + 1):
            other(k)
        for c in sent[mark:]:
            c.wait_send()
        del sent[mark:]

    @pl.when(s == 1)
    def _():
        def piece(zz, hh):
            return rows.at[hh, zz, 1]

        mark = len(sent)
        b = rows.at[yh, z, 1, t]
        for oy in (0, 1, 3, 2):
            for ox in range(NX):
                if oy + ox:
                    n = oy * NX + ox
                    start(_remote(b, b, ssend.at[n], srecv.at[n], xy_dev((x + ox) % NX, (y + oy) % NY)))

        def to_partner(p, i):
            start(_remote(p, p, psend.at[i], precv.at[i], partner))

        def other(i, *xx):
            for e in xx:
                for j in range(4):
                    yy = ymine[j]
                    landed(rows.at[yy // 2, :, 0, (yy % 2) * NX + e], precv.at[4 * i + j])
                i = i + 1
            use_group(*xx)

        def out(j):
            q = quad_of(z, ymine[j])
            start(_remote(q, q, rsend.at[0, j], rrecv.at[0, j], z_dev(zr)))
            start(_remote(q, q, rsend.at[1, j], rrecv.at[1, j], z_dev(zl)))
            to_partner(q, qid(0, 0, j))

        def ring_in(k, j):
            n = 4 * k + j
            for way in range(2):
                if k == half and j % 2 != way:
                    continue
                q = quad_of((z + NZ - k if way == 0 else z + k) % NZ, ymine[j])
                landed(q, rrecv.at[way, n - 4])
                if k < half - 1 or (k == half - 1 and j % 2 == way):
                    start(_remote(q, q, rsend.at[way, n], rrecv.at[way, n], z_dev((zr, zl)[way])))
                to_partner(q, qid(k, 0 if k == half else way, j))

        for j, oy in enumerate((0, 1, 3, 2)):
            yy = ymine[j]
            for ox in range(NX):
                if oy + ox:
                    n = oy * NX + ox
                    landed(rows.at[yy // 2, z, 1, (yy % 2) * NX + (x + NX - ox) % NX], srecv.at[n])
            out(j)
        use_plane(0)
        for k in range(1, half + 1):
            for j in range(4):
                ring_in(k, j)
            if k < half:
                use_plane(k)
            if k == 2:
                other(0, x)
            if k == 3:
                other(1, xl, xr)
        use_plane(half)
        other(3, xo)
        for c in sent[mark:]:
            c.wait_send()
        del sent[mark:]

    gate = hacc[:, :, :, :128].reshape(NST * BR, 128)
    up = hacc[:, :, :, 128:].reshape(NST * BR, 128)
    weight = wcol[:, 0:1]
    hid[...] = (weight * (gate / (1.0 + jnp.exp(-gate))) * up).astype(BF16).reshape(2, NT, BR, 128)

    def down_plane(dst, sec, zz, hh):
        a = hid[sec].reshape(NT * BR, 128)
        p = jnp.dot(a, wdbuf[hh * NZ + zz], preferred_element_type=F32)
        for e in range(NT):
            put(dst.at[hh, zz, e], p[BR * e : BR * (e + 1)])

    def down_group(dst, sec, *xx):
        places = [o + e for e in xx for o in (0, NX)]
        a = jnp.concatenate([hid[sec, e] for e in places], axis=0)

        def step(i, carry):
            p = jnp.dot(a, wdbuf[i], preferred_element_type=F32)
            for n, e in enumerate(places):
                put(dst.at[i // NZ, i % NZ, e], p[n * BR : (n + 1) * BR])
            return carry

        lax.fori_loop(0, NG, step, 0)

    def add(dst, srcs, n=8):
        def step(i, carry):
            v = dst[i].astype(F32)
            for r in srcs:
                v = v + r[i].astype(F32)
            dst[i] = v.astype(BF16)
            return carry

        lax.fori_loop(0, n, step, 0)

    def finish(refs):
        tot = refs[0][...].astype(F32)
        for r in refs[1:]:
            tot = tot + r[...].astype(F32)
        tot = mine[...].astype(F32) + tot
        for r in range(2):
            for c in range(3):
                n = TILE * (3 * r + c)
                out_ref[TILE * r : TILE * (r + 1), 128 * c : 128 * (c + 1)] = tot[n : n + TILE].astype(BF16)
        tails = tot[6 * TILE :]
        out_ref[:TILE, 384:] = tails[:, :64].astype(BF16)
        out_ref[TILE:, 384:] = pltpu.roll(tails, 64, 1)[:, :64].astype(BF16)

    xs = (xo, xr, xl, x)
    zs = [(z + half) % NZ]
    for k in range(half - 1, 0, -1):
        zs += [(z + k) % NZ, (z + NZ - k) % NZ]
    zs.append(z)
    ys = ((y + 2) % NY, (y + 1) % NY, (y + NY - 1) % NY, y)
    yright, yleft = y_dev((y + 1) % NY), y_dev((y + NY - 1) % NY)

    def quad(ref, i, j):
        return ref.at[ys[j] // 2, zs[i], pl.ds((ys[j] % 2) * NX, NX)]

    @pl.when(s == 0)
    def _():
        mark = len(sent)

        def give(i):
            for h in range(2):
                down_plane(tsend, 1, zs[i], h)
            for j in range(4):
                n = 4 * i + j
                start(_remote(quad(tsend, i, j), quad(pbuf, i, j), cpsend.at[n], cprecv.at[n], partner))

        def at(ref, i, j):
            yy = ys[j]
            return ref.at[yy // 2, :, (yy % 2) * NX + xs[i]]

        def take(i, j, more=()):
            landed(at(pbuf, i, j), cprecv.at[4 * i + j])
            add(at(acc, i, j), [at(pbuf, i, j)] + list(more))

        right, left = x_dev(xr), x_dev(xl)
        give(0)
        down_group(acc, 0, xs[0])
        give(1)
        for j in range(4):
            take(0, j)
            start(_remote(at(acc, 0, j), ring.at[j], crsend.at[j], crrecv.at[j], right if j % 2 == 0 else left))
        down_group(acc, 0, xs[1])
        give(2)
        down_group(acc, 0, xs[2])
        give(3)
        for j in range(4):
            for i, way, dev in ((1, 0, right), (2, 1, left)):
                if j % 2 == way:
                    landed(ring.at[j], crrecv.at[j])
                    take(i, j, [ring.at[j]])
                else:
                    take(i, j)
                k = 4 + 4 * way + j
                start(_remote(at(acc, i, j), ring.at[k], crsend.at[k], crrecv.at[k], dev))
            give(4 + j)
        down_group(acc, 0, xs[3])
        for j in range(4):
            landed(ring.at[4 + j], crrecv.at[4 + j])
            landed(ring.at[8 + j], crrecv.at[8 + j])
            take(3, j, [ring.at[4 + j], ring.at[8 + j]])
            yy = ys[j]
            tt = (yy % 2) * NX + x
            if j == 0:
                for w in range(2):
                    part4 = pl.ds(4 * w, 4)
                    start(
                        _remote(
                            acc.at[yy // 2, part4, tt],
                            ybuf.at[0, part4],
                            cysend.at[w],
                            cyrecv.at[w],
                            (yright, yleft)[w],
                        )
                    )
            elif j < 3:
                w = j - 1
                part4 = pl.ds(4 * w, 4)
                landed(ybuf.at[0, part4], cyrecv.at[w])
                add(acc.at[yy // 2, part4, tt], [ybuf.at[0, part4]], 4)
                start(
                    _remote(at(acc, 3, j), ybuf.at[j], cysend.at[1 + j], cyrecv.at[1 + j], (yright, yleft)[w])
                )
        for j in (1, 2):
            landed(ybuf.at[j], cyrecv.at[1 + j])
        add(at(acc, 3, 3), [ybuf.at[1], ybuf.at[2]])
        for o in range(1, NZ):
            e = (z + o) % NZ
            start(_remote(acc.at[yh, e, t], fbuf.at[o], cfsend.at[o], cfrecv.at[o], z_dev(e)))
        for o in range(1, NZ):
            landed(fbuf.at[o], cfrecv.at[o])
        finish([acc.at[yh, z, t]] + [fbuf.at[o] for o in range(1, NZ)])
        for c in sent[mark:]:
            c.wait_send()
        del sent[mark:]

    @pl.when(s == 1)
    def _():
        mark = len(sent)

        def give(*ii):
            down_group(tsend, 0, *[xs[i] for i in ii])
            for j, yy in enumerate(ys):
                for i in ii:
                    tt = (yy % 2) * NX + xs[i]
                    n = 4 * i + j
                    start(
                        _remote(
                            tsend.at[yy // 2, :, tt], pbuf.at[yy // 2, :, tt], cpsend.at[n], cprecv.at[n], partner
                        )
                    )

        def have(i):
            for h in range(2):
                down_plane(acc, 1, zs[i], h)

        def take(i, j, more=()):
            landed(quad(pbuf, i, j), cprecv.at[4 * i + j])
            add(quad(acc, i, j), [quad(pbuf, i, j)] + list(more), NX)

        def slot(n):
            return ring.at[n // 2, pl.ds((n % 2) * NX, NX)]

        right, left = z_dev(zr), z_dev(zl)
        give(0)
        have(0)
        for j in range(4):
            take(0, j)
            start(_remote(quad(acc, 0, j), slot(j), crsend.at[j], crrecv.at[j], (right, left)[j % 2]))
        have(1)
        have(2)
        give(1, 2)
        for k in range(1, half):
            for j in range(4):
                for way, dev in ((0, right), (1, left)):
                    i = 2 * k - 1 + way
                    prev = 4 + 8 * (k - 2) + 4 * way + j
                    if k == 1:
                        prev = j if j % 2 == way else None
                    if prev is None:
                        take(i, j)
                    else:
                        landed(slot(prev), crrecv.at[prev])
                        take(i, j, [slot(prev)])
                    q = 4 + 8 * (k - 1) + 4 * way + j
                    start(_remote(quad(acc, i, j), slot(q), crsend.at[q], crrecv.at[q], dev))
            if k == 1:
                give(3)
            have(2 * k + 1)
            if k < half - 1:
                have(2 * k + 2)

        for j in range(4):
            q = 4 + 8 * (half - 2) + j
            landed(slot(q), crrecv.at[q])
            landed(slot(q + 4), crrecv.at[q + 4])
            take(7, j, [slot(q), slot(q + 4)])
            oy = (2, 1, 3, 0)[j]
            for ox in range(NX):
                if oy + ox:
                    n = oy * NX + ox
                    ex = (x + ox) % NX
                    src = acc.at[ys[j] // 2, z, (ys[j] % 2) * NX + ex]
                    start(_remote(src, fbuf.at[n], cfsend.at[n], cfrecv.at[n], xy_dev(ex, ys[j])))
        for n in range(1, NY * NX):
            landed(fbuf.at[n], cfrecv.at[n])
        finish([acc.at[yh, z, t]] + [fbuf.at[n] for n in range(1, NY * NX)])
        for c in sent[mark:]:
            c.wait_send()
        del sent[mark:]

    for o in range(1, NST):
        e = (d + o) % NST
        _remote(part.at[e], rbuf.at[d], bsend.at[e], brecv.at[d], st_dev(e)).wait_send()
    for c in sent:
        c.wait_send()


def layer(queries, latent_cache, cache_len, value_up, out_proj, residual, w_gate, w_up, w_down, route_ids, route_weights):
    vmem = pl.BlockSpec(memory_space=pltpu.VMEM)
    hbm = pl.BlockSpec(memory_space=pl.ANY)
    dma = pltpu.SemaphoreType.DMA
    depth = value_up.shape[0] * VDIM
    scratch = [
        pltpu.VMEM((BR, latent_cache.shape[2], latent_cache.shape[1]), BF16),
        pltpu.VMEM(value_up.shape, BF16),
        pltpu.VMEM((BR // 2, queries.shape[1], latent_cache.shape[1]), F32),
        pltpu.VMEM((BR // 2, queries.shape[1], LAT), F32),
        pltpu.VMEM((2, BR // 2, depth), BF16),
        pltpu.VMEM((NG, 2, BR // 2, depth), BF16),
        pltpu.VMEM((depth, BC), BF16),
        pltpu.VMEM((NG, WIDE, 256), BF16),
        pltpu.VMEM(w_down.shape, BF16),
        pltpu.VMEM((NG, 128, WIDE), BF16),
        pltpu.VMEM((128, BC), BF16),
        pltpu.VMEM((NST * BR, 8), F32),
        pltpu.VMEM((NST, BR, BC), BF16),
        pltpu.VMEM((NST, BR, BC), BF16),
        pltpu.VMEM((PACK, 128), BF16),
        pltpu.VMEM((2, NZ, 2, NT, PACK, 128), BF16),
        pltpu.VMEM((2, NT, BR, 256), F32),
        pltpu.VMEM((2, NT, BR, 128), BF16),
        pltpu.VMEM((2, NZ, NT, PACK, 128), BF16),
        pltpu.VMEM((2, NZ, NT, PACK, 128), BF16),
        pltpu.VMEM((2, NZ, NT, PACK, 128), BF16),
        pltpu.VMEM((16, 8, PACK, 128), BF16),
        pltpu.VMEM((3, 8, PACK, 128), BF16),
        pltpu.VMEM((16, PACK, 128), BF16),
        pltpu.VMEM((BR, WIDE), F32),
        dma((3,)),
        dma((5,)),
        dma((NG, 2, 5)),
        dma((NG, 2)),
        dma((1,)),
        dma((NST,)),
        dma((NST,)),
        dma((16,)),
        dma((16,)),
        dma((NY,)),
        dma((NY,)),
        dma((2, 16)),
        dma((2, 16)),
        dma((32,)),
        dma((32,)),
        dma((32,)),
        dma((32,)),
        dma((28,)),
        dma((28,)),
        dma((4,)),
        dma((4,)),
        dma((16,)),
        dma((16,)),
    ]
    return pl.pallas_call(
        _layer_kernel,
        out_shape=jax.ShapeDtypeStruct((BR, BC), BF16),
        in_specs=[pl.BlockSpec(memory_space=pltpu.SMEM), vmem, hbm, hbm, vmem, vmem, hbm, hbm, hbm, vmem, vmem],
        out_specs=vmem,
        scratch_shapes=scratch,
        compiler_params=pltpu.CompilerParams(
            collective_id=0, has_side_effects=True, vmem_limit_bytes=60 * 1024 * 1024
        ),
        name="layer",
    )(
        cache_len,
        queries,
        latent_cache.transpose(0, 2, 1),
        value_up,
        out_proj.T,
        residual.T,
        w_gate.reshape(NG, BC, 128),
        w_up.reshape(NG, BC, 128),
        w_down,
        route_ids.T,
        route_weights.T,
    )


def on_device(
    queries,
    latent_cache,
    cache_len,
    value_up,
    out_proj,
    residual,
    w_gate,
    w_up,
    w_down,
    route_ids,
    route_weights,
):
    return layer(
        queries,
        latent_cache,
        cache_len,
        value_up,
        out_proj,
        residual,
        w_gate[0],
        w_up[0],
        w_down[0],
        route_ids,
        route_weights,
    )


def solution(mesh):
    return jax.shard_map(
        on_device,
        mesh=mesh,
        in_specs=(
            P("grp", ("sect", "tp"), None),
            P("grp", None, None),
            P("grp"),
            P(("sect", "tp"), None, None),
            P(("sect", "tp"), "grp"),
            P(None, "grp"),
            P("grp", None, ("sect", "tp")),
            P("grp", None, ("sect", "tp")),
            P("grp", ("sect", "tp"), None),
            P(),
            P(),
        ),
        out_specs=P(("sect", "tp"), "grp"),
        check_vma=False,
    )
```
